128 devices in a mesh: prefix: 8 (over z_lo, y), cand: 16 (over x, z_hi, core).
Axes of the slice: x: 4, y: 4, z: 4 (z_hi: 2, z_lo: 2; z = z_hi * 2 + z_lo), core: 2. Of those that a mesh axis runs over, the one named last changes fastest.
Arguments:
- query: bfloat16 [4096, 8192], P('cand', 'prefix'), may hold values from -100 to 100
- grad_out: bfloat16 [4096, 8192], P('cand', 'prefix'), may hold values from -24 to 24
- continuation_key: bfloat16 [4096, 1024], P('cand', 'prefix'), may hold values from -8 to 8
- continuation_value: bfloat16 [4096, 1024], P('cand', 'prefix'), may hold values from -6 to 6
- prompt_key: bfloat16 [3072, 1024], P(('prefix', 'cand')), may hold values from -4 to 4
- shared_prompt_value: bfloat16 [3072, 1024], P(('prefix', 'cand')), may hold values from -6 to 6
- assign: int32 [64], replicated, may hold values from 0 to 15, as said below
- lengths: int32 [64], replicated, may hold values from 1 to 64, as said below
- offsets: int32 [64], replicated, may hold values from 1536 to 3072
Outputs:
- query_grad: bfloat16 [4096, 8192], P('cand', 'prefix')
- cont_key_grad: bfloat16 [4096, 1024], P('cand', 'prefix')
- cont_value_grad: bfloat16 [4096, 1024], P('cand', 'prefix')
- prompt_key_grad: bfloat16 [3072, 1024], P(('prefix', 'cand'))
- prompt_value_grad: bfloat16 [3072, 1024], P(('prefix', 'cand'))
The draws below stay inside these ranges and needn't reach their ends.
Inputs may be any that keep to these rules, and one draw needn't show every extreme that they name: `assign`: each index of cand is named by exactly 4 candidates. The lengths of the candidates on one index of cand sum to at most 256; on some index they sum to exactly 256, each of its candidates having length 64.
All inputs are finite; a program needn't handle non-finite values.
Results may differ from the reference program's by a relative error of at most 0.015.
Values may be sent and summed in bfloat16 or wider, within the bound.
A program may use at most 64 MiB of HBM per device.

```python
import math
import jax
import jax.numpy as jnp
from jax import lax

QUERY_HEAD_COUNT = 64
KEY_VALUE_HEADS = 8
HEAD_WIDTH = 128
CPD = 4
NCAND = 64
ROWS_DEV = 256
CONT_ROW_SLOTS = 4096
PROMPT_TOKENS = 3072
N_CAND = 16


def layout_draw(key):
    device_count = NCAND // CPD
    cand_order = jax.random.permutation(jax.random.fold_in(key, 81), NCAND)
    assign = (cand_order // CPD).astype(jnp.int32)
    length_cap = ROWS_DEV // CPD
    drawn = jax.random.randint(jax.random.fold_in(key, 82), (NCAND,), 1, length_cap + 1)
    full_device = jax.random.randint(jax.random.fold_in(key, 83), (), 0, device_count)
    lengths = jnp.where(assign == full_device, length_cap, drawn).astype(jnp.int32)
    return (assign, lengths)


def draw_assign(key, part):
    return layout_draw(key)[0]


def draw_lengths(key, part):
    return layout_draw(key)[1]


def draw_offsets(key, part):
    lowest = PROMPT_TOKENS // 2
    drawn = jax.random.randint(jax.random.fold_in(key, 91), (NCAND,), lowest, PROMPT_TOKENS + 1)
    chosen = jax.random.permutation(jax.random.fold_in(key, 92), NCAND)
    cand_index = jnp.arange(NCAND)
    drawn = jnp.where(cand_index == chosen[0], PROMPT_TOKENS, drawn)
    drawn = jnp.where(cand_index == chosen[1], lowest, drawn)
    return drawn.astype(jnp.int32)


def draw_prompt_key(key, part):
    starting_sample = jax.random.truncated_normal(jax.random.fold_in(key, 72), -4.0, 4.0, (PROMPT_TOKENS, KEY_VALUE_HEADS * HEAD_WIDTH), jnp.float32)
    return starting_sample.astype(jnp.bfloat16)


def draw_query(key, part):
    starting_sample = 2.0 * jax.random.truncated_normal(jax.random.fold_in(key, 73), -4.0, 4.0, (CONT_ROW_SLOTS, QUERY_HEAD_COUNT * HEAD_WIDTH), jnp.float32)
    return starting_sample.astype(jnp.bfloat16)


def block_scale(stream_key, shape, pieces, least, largest):
    level = 1.0
    for position, shards_of in pieces:
        heights = jax.random.uniform(jax.random.fold_in(jax.random.fold_in(stream_key, 6), position), (shards_of,), jnp.float32, least / len(pieces), largest / len(pieces))
        level = level * jnp.repeat(jnp.exp(heights), shape[position] // shards_of).reshape((-1,) + (1,) * (len(shape) - 1 - position))
    return level


def normal_values(own_key, shape, scale, limit, cuts=(), held_as=jnp.bfloat16):
    values = scale * jax.random.normal(own_key, shape, jnp.float32)
    if cuts:
        values = values * block_scale(own_key, shape, cuts, -0.22, 0.18)
    return jnp.clip(values, -limit, limit).astype(held_as)


def setup_inputs(seed: int = 0) -> dict:
    splits = jax.random.split(jax.random.key(seed), 10)
    query = draw_query(jax.random.fold_in(splits[9], 71), 0)
    grad_out = normal_values(splits[1], (CONT_ROW_SLOTS, QUERY_HEAD_COUNT * HEAD_WIDTH), 4.0, 24.0, ((0, 16), (1, 8)))
    continuation_key = normal_values(splits[2], (CONT_ROW_SLOTS, KEY_VALUE_HEADS * HEAD_WIDTH), 1.5, 8.0, ((0, 16), (1, 8)))
    continuation_value = normal_values(splits[3], (CONT_ROW_SLOTS, KEY_VALUE_HEADS * HEAD_WIDTH), 1.0, 6.0, ((0, 16), (1, 8)))
    prompt_key = draw_prompt_key(jax.random.fold_in(splits[9], 71), 0)
    shared_prompt_value = normal_values(splits[5], (PROMPT_TOKENS, KEY_VALUE_HEADS * HEAD_WIDTH), 1.0, 6.0, ((0, 128),))
    assign = draw_assign(jax.random.fold_in(splits[9], 71), 0)
    lengths = draw_lengths(jax.random.fold_in(splits[9], 71), 0)
    offsets = draw_offsets(jax.random.fold_in(splits[9], 71), 0)
    return dict(query=query, grad_out=grad_out, continuation_key=continuation_key, continuation_value=continuation_value, prompt_key=prompt_key, shared_prompt_value=shared_prompt_value, assign=assign, lengths=lengths, offsets=offsets)


MASKED_SCORE = -1e+30
HIGHEST = lax.Precision.HIGHEST

def slot_layout(assign, lengths, offsets, device, slot_count):
    cand_count = assign.shape[0]
    cand_order = jnp.arange(cand_count, dtype=jnp.int32)
    earlier_same = (assign[:, None] == assign[None, :]) & (cand_order[None, :] < cand_order[:, None])
    starts = lax.optimization_barrier(jnp.sum(jnp.where(earlier_same, lengths[None, :], 0), axis=1)).astype(jnp.int32)
    slot_index = jnp.arange(slot_count, dtype=jnp.int32)
    slot_match = (assign[:, None] == device) & (slot_index[None, :] >= starts[:, None]) & (slot_index[None, :] < (starts + lengths)[:, None])
    row_valid = jnp.any(slot_match, axis=0)
    row_segment = lax.optimization_barrier(jnp.sum(jnp.where(slot_match, cand_order[:, None], 0), axis=0)).astype(jnp.int32)
    offset_row = lax.optimization_barrier(jnp.sum(jnp.where(slot_match, offsets[:, None], 0), axis=0)).astype(jnp.int32)
    return (row_valid, row_segment, offset_row)

def attend(queries, grad_rows, joined_keys, joined_values, key_segment, key_position, row_valid, row_segment, offset_row):
    row_count = queries.shape[0]
    head_count = joined_keys.shape[1]
    head_size = joined_keys.shape[2]
    key_count = joined_keys.shape[0]
    block_size = math.gcd(key_count, 256)
    block_count = key_count // block_size
    score_scale = 1.0 / math.sqrt(head_size)
    query_heads = queries.reshape(row_count, head_count, -1, head_size).astype(jnp.float32)
    grad_heads = grad_rows.reshape(query_heads.shape).astype(jnp.float32)
    slot_index = jnp.arange(row_count, dtype=jnp.int32)
    stacked = (joined_keys.reshape(block_count, block_size, head_count, head_size), joined_values.reshape(block_count, block_size, head_count, head_size), key_segment.reshape(block_count, block_size), key_position.reshape(block_count, block_size))

    def scores(block_items):
        key_block, value_block, block_segment, block_position = block_items
        prompt_ok = (block_segment[None, :] == -1) & (block_position[None, :] < offset_row[:, None])
        cont_ok = (block_segment[None, :] == row_segment[:, None]) & (block_position[None, :] <= slot_index[:, None])
        visible_mask = (row_valid[:, None] & (prompt_ok | cont_ok))[None, None]
        raw_scores = jnp.einsum('rhgd,jhd->hgrj', query_heads, key_block.astype(jnp.float32), precision=HIGHEST) * score_scale
        return (raw_scores, visible_mask)

    def normaliser(state_pair, block_items):
        running_max, summed = state_pair
        raw_scores, visible_mask = scores(block_items)
        fresh_max = jnp.maximum(running_max, lax.optimization_barrier(jnp.max(jnp.where(visible_mask, raw_scores, MASKED_SCORE), axis=3)))
        summed = summed * jnp.exp(running_max - fresh_max) + lax.optimization_barrier(jnp.sum(jnp.where(visible_mask, jnp.exp(raw_scores - fresh_max[..., None]), 0.0), axis=3))
        return ((fresh_max, summed), None)
    stat_shape = (head_count, query_heads.shape[2], row_count)
    start_pair = (jnp.full(stat_shape, MASKED_SCORE, jnp.float32), jnp.zeros(stat_shape, jnp.float32))
    (running_max, summed), _ = lax.scan(normaliser, start_pair, stacked)
    lse = running_max + jnp.log(jnp.where(row_valid[None, None, :], summed, 1.0))

    def weighting(raw_scores, visible_mask):
        return jnp.where(visible_mask, jnp.exp(raw_scores - lse[..., None]), 0.0)

    def forward(attended, block_items):
        raw_scores, visible_mask = scores(block_items)
        probs_bf = weighting(raw_scores, visible_mask).astype(jnp.bfloat16).astype(jnp.float32)
        value_block = block_items[1].astype(jnp.float32)
        return (attended + jnp.einsum('hgrj,jhd->rhgd', probs_bf, value_block, precision=HIGHEST), None)
    attended, _ = lax.scan(forward, jnp.zeros(query_heads.shape, jnp.float32), stacked)
    row_delta = jnp.transpose(lax.optimization_barrier(jnp.sum(grad_heads * attended, axis=3)), (1, 2, 0))

    def backward(grad_query, block_items):
        raw_scores, visible_mask = scores(block_items)
        weights = weighting(raw_scores, visible_mask)
        probs_bf = weights.astype(jnp.bfloat16).astype(jnp.float32)
        key_block = block_items[0].astype(jnp.float32)
        value_block = block_items[1].astype(jnp.float32)
        prob_grad = jnp.einsum('rhgd,jhd->hgrj', grad_heads, value_block, precision=HIGHEST)
        score_grad = (weights * (prob_grad - row_delta[..., None])).astype(jnp.bfloat16).astype(jnp.float32)
        value_sum = jnp.einsum('hgrj,rhgd->jhd', probs_bf, grad_heads, precision=HIGHEST)
        key_sum = jnp.einsum('hgrj,rhgd->jhd', score_grad, query_heads, precision=HIGHEST) * score_scale
        grad_query = grad_query + jnp.einsum('hgrj,jhd->rhgd', score_grad, key_block, precision=HIGHEST)
        return (grad_query, (key_sum, value_sum))
    grad_query, (key_sums, value_sums) = lax.scan(backward, jnp.zeros(query_heads.shape, jnp.float32), stacked)
    return (grad_query * score_scale, key_sums.reshape(key_count, head_count, head_size), value_sums.reshape(key_count, head_count, head_size))

def rounded_part(values):
    narrow = lax.optimization_barrier(values.astype(jnp.bfloat16))
    return narrow.astype(jnp.float32)

def reference(query, grad_out, continuation_key, continuation_value, prompt_key, shared_prompt_value, assign, lengths, offsets):
    row_count = query.shape[0] // N_CAND
    prompt_len = prompt_key.shape[0]
    head_count = prompt_key.shape[1] // HEAD_WIDTH
    prompt_keys = prompt_key.reshape(prompt_len, head_count, HEAD_WIDTH)
    prompt_values = shared_prompt_value.reshape(prompt_len, head_count, HEAD_WIDTH)

    def per_device(state_pair, device):
        first_row = device * row_count
        queries = lax.dynamic_slice_in_dim(query, first_row, row_count, 0)
        grad_rows = lax.dynamic_slice_in_dim(grad_out, first_row, row_count, 0)
        cont_keys = lax.dynamic_slice_in_dim(continuation_key, first_row, row_count, 0).reshape(row_count, head_count, HEAD_WIDTH)
        cont_values = lax.dynamic_slice_in_dim(continuation_value, first_row, row_count, 0).reshape(row_count, head_count, HEAD_WIDTH)
        row_valid, row_segment, offset_row = slot_layout(assign, lengths, offsets, device, row_count)
        joined_keys = jnp.concatenate([prompt_keys, cont_keys], axis=0)
        joined_values = jnp.concatenate([prompt_values, cont_values], axis=0)
        key_segment = jnp.concatenate([jnp.full((prompt_len,), -1, jnp.int32), jnp.where(row_valid, row_segment, -2).astype(jnp.int32)])
        key_position = jnp.concatenate([jnp.arange(prompt_len, dtype=jnp.int32), jnp.arange(row_count, dtype=jnp.int32)])
        grad_query, key_sums, value_sums = attend(queries, grad_rows, joined_keys, joined_values, key_segment, key_position, row_valid, row_segment, offset_row)
        new_pair = (state_pair[0] + rounded_part(key_sums[:prompt_len]), state_pair[1] + rounded_part(value_sums[:prompt_len]))
        outputs = (grad_query.reshape(row_count, -1).astype(jnp.bfloat16), key_sums[prompt_len:].reshape(row_count, -1).astype(jnp.bfloat16), value_sums[prompt_len:].reshape(row_count, -1).astype(jnp.bfloat16))
        return (new_pair, outputs)
    zero_grad = jnp.zeros((prompt_len, head_count, HEAD_WIDTH), jnp.float32)
    (key_total, value_total), (query_grads, key_grads, value_grads) = lax.scan(per_device, (zero_grad, zero_grad), jnp.arange(N_CAND, dtype=jnp.int32))
    return (query_grads.reshape(query.shape[0], -1), key_grads.reshape(query.shape[0], -1), value_grads.reshape(query.shape[0], -1), key_total.reshape(prompt_len, -1).astype(jnp.bfloat16), value_total.reshape(prompt_len, -1).astype(jnp.bfloat16))
```

```python
import functools
import math

import jax
import jax.numpy as jnp
from jax import lax
from jax.experimental import pallas as pl
from jax.experimental.pallas import tpu as pltpu
from jax.sharding import PartitionSpec as P

D = 128
MESH = pl.DeviceIdType.MESH
ALL, LOW, HIGH = pl.ds(0, 8), pl.ds(0, 4), pl.ds(4, 4)


def place():
    p, c = lax.axis_index("prefix"), lax.axis_index("cand")
    x, zh, co = c // 4, (c // 2) % 2, c % 2
    right, left, opp = (x + 1) % 4, (x + 3) % 4, (x + 2) % 4
    at = lambda xx, zz, cc: (p, xx * 4 + zz * 2 + cc)
    peers = {"R": at(right, zh, co), "L": at(left, zh, co), "Z": at(x, 1 - zh, co), "C": at(x, zh, 1 - co)}
    return p, c, x, zh, co, right, left, opp, peers


def greet(p, c, peers):
    barrier = pltpu.get_barrier_semaphore()
    ring = [((p + d) % 8, c) for d in range(1, 8)]
    everyone = ring + list(peers.values())
    for peer in everyone:
        pl.semaphore_signal(barrier, inc=1, device_id=peer, device_id_type=MESH)
    pl.semaphore_wait(barrier, len(everyone))


class Links:
    def __init__(self, send, recv):
        self.send, self.recv, self.n, self.started = send, recv, 0, []

    def make(self, src, dst, peer, slot=None):
        i = self.n
        self.n += 1
        return pltpu.make_async_remote_copy(src_ref=src, dst_ref=dst, send_sem=self.send.at[i], recv_sem=self.recv.at[i],
                                            device_id=peer, device_id_type=MESH)


N_GATHER = 64


def gather_kernel(pk, pv, fk, fv, send, recv, own_sem):
    p, c, x, zh, co, right, left, opp, peers = place()
    links = Links(send, recv)
    greet(p, c, peers)
    full = (fk, fv)
    sent = []

    first = [[], []]
    own = []
    for a, (src, dst) in enumerate(((pk, fk), (pv, fv))):
        for d in range(1, 8):
            q = (p + d) % 8
            cp = links.make(src.at[:, pl.ds(pl.multiple_of(q * D, D), D)], dst.at[p, x, zh, co], (q, c))
            cp.start()
            first[a].append(cp)
        cp = pltpu.make_async_copy(src.at[:, pl.ds(pl.multiple_of(p * D, D), D)], dst.at[p, x, zh, co], own_sem.at[a])
        cp.start()
        own.append(cp)

    def ship(a, half, xx, zz, who):
        ref = full[a].at[half, xx, zz, co]
        cp = links.make(ref, ref, peers[who])
        cp.start()
        sent.append(cp)
        return cp

    pending_core = []

    def core(a, half, xx, zz):
        pending_core.append(ship(a, half, xx, zz, "C"))

    for cp in first[0]:
        cp.wait_recv()
    own[0].wait()
    kz = ship(0, ALL, x, zh, "Z")
    kr = ship(0, ALL, x, zh, "R")
    kl = ship(0, ALL, x, zh, "L")
    core(0, ALL, x, zh)
    for cp in first[1]:
        cp.wait_recv()
    own[1].wait()
    vr = ship(1, ALL, x, zh, "R")
    vl = ship(1, ALL, x, zh, "L")
    vz = ship(1, ALL, x, zh, "Z")
    core(1, ALL, x, zh)
    kr.wait_recv()
    kr2 = ship(0, LOW, left, zh, "R")
    core(0, ALL, left, zh)
    kl.wait_recv()
    kl2 = ship(0, HIGH, right, zh, "L")
    core(0, ALL, right, zh)
    vr.wait_recv()
    vr2 = ship(1, LOW, left, zh, "R")
    vz2 = ship(1, ALL, left, zh, "Z")
    core(1, ALL, left, zh)
    vl.wait_recv()
    vl2 = ship(1, HIGH, right, zh, "L")
    vz3 = ship(1, ALL, right, zh, "Z")
    core(1, ALL, right, zh)
    kz.wait_recv()
    zr = ship(0, ALL, x, 1 - zh, "R")
    zl = ship(0, ALL, x, 1 - zh, "L")
    core(0, ALL, x, 1 - zh)
    kr2.wait_recv()
    core(0, LOW, opp, zh)
    kl2.wait_recv()
    core(0, HIGH, opp, zh)
    vr2.wait_recv()
    vz4 = ship(1, LOW, opp, zh, "Z")
    core(1, LOW, opp, zh)
    vl2.wait_recv()
    vz5 = ship(1, HIGH, opp, zh, "Z")
    core(1, HIGH, opp, zh)
    zr.wait_recv()
    zr2 = ship(0, LOW, left, 1 - zh, "R")
    core(0, ALL, left, 1 - zh)
    zl.wait_recv()
    zl2 = ship(0, HIGH, right, 1 - zh, "L")
    core(0, ALL, right, 1 - zh)
    vz.wait_recv()
    core(1, ALL, x, 1 - zh)
    vz2.wait_recv()
    core(1, ALL, left, 1 - zh)
    vz3.wait_recv()
    core(1, ALL, right, 1 - zh)
    zr2.wait_recv()
    core(0, LOW, opp, 1 - zh)
    zl2.wait_recv()
    core(0, HIGH, opp, 1 - zh)
    vz4.wait_recv()
    core(1, LOW, opp, 1 - zh)
    vz5.wait_recv()
    core(1, HIGH, opp, 1 - zh)
    for cp in pending_core:
        cp.wait_recv()
    for cp in first[0] + first[1] + sent:
        cp.wait_send()


def gather(pk, pv):
    rows = pk.shape[0]
    out = jax.ShapeDtypeStruct((8, 4, 2, 2, rows, D), pk.dtype)
    anyspace = pl.BlockSpec(memory_space=pl.ANY)
    fk, fv = pl.pallas_call(
        gather_kernel,
        out_shape=(out, out),
        in_specs=[anyspace] * 2,
        out_specs=[anyspace] * 2,
        scratch_shapes=[pltpu.SemaphoreType.DMA((N_GATHER,)), pltpu.SemaphoreType.DMA((N_GATHER,)), pltpu.SemaphoreType.DMA((2,))],
        compiler_params=pltpu.CompilerParams(collective_id=0, has_side_effects=True),
    )(pk, pv)
    return fk.reshape(-1, D), fv.reshape(-1, D)


def add(a, b):
    return (a.astype(jnp.float32) + b.astype(jnp.float32)).astype(a.dtype)


def reduce_kernel(dk, dv, ok, ov, ks, vs, kc, vc, kxl, kxr, kl, kr, kz, vz, vxl, vxr, vl, vr, okb, ovb, send, recv, own_sem):
    p, c, x, zh, co, right, left, opp, peers = place()
    links = Links(send, recv)
    greet(p, c, peers)
    sent = []

    def ship(src, dst, who):
        cp = links.make(src, dst, peers[who])
        cp.start()
        sent.append(cp)
        return cp

    other = 1 - zh
    kc_in, vc_in = {}, {}
    kc_in["opp"] = ship(dk.at[:, opp, :, 1 - co], kc.at[:, opp], "C")
    vc_in["other"] = ship(dv.at[:, :, other, 1 - co], vc.at[:, :, other], "C")
    kc_in["right"] = ship(dk.at[:, right, :, 1 - co], kc.at[:, right], "C")
    kc_in["left"] = ship(dk.at[:, left, :, 1 - co], kc.at[:, left], "C")
    vc_in["own"] = ship(dv.at[:, :, zh, 1 - co], vc.at[:, :, zh], "C")
    kc_in["own"] = ship(dk.at[:, x, :, 1 - co], kc.at[:, x], "C")

    kc_in["opp"].wait_recv()
    ks[:, opp] = add(dk[:, opp, :, co], kc[:, opp])
    k1 = ship(ks.at[LOW, opp], kxl, "R")
    k2 = ship(ks.at[HIGH, opp], kxr, "L")
    vc_in["other"].wait_recv()
    vs[:, :, other] = add(dv[:, :, other, co], vc[:, :, other])
    z1 = ship(vs.at[:, :, other], vz, "Z")
    kc_in["right"].wait_recv()
    k1.wait_recv()
    both = dk[:, right, :, co].astype(jnp.float32) + kc[:, right].astype(jnp.float32)
    ks[LOW, right] = (both[:4] + kxl[...].astype(jnp.float32)).astype(ks.dtype)
    ks[HIGH, right] = both[4:].astype(ks.dtype)
    k3 = ship(ks.at[:, right], kl, "R")
    kc_in["left"].wait_recv()
    k2.wait_recv()
    both = dk[:, left, :, co].astype(jnp.float32) + kc[:, left].astype(jnp.float32)
    ks[LOW, left] = both[:4].astype(ks.dtype)
    ks[HIGH, left] = (both[4:] + kxr[...].astype(jnp.float32)).astype(ks.dtype)
    k4 = ship(ks.at[:, left], kr, "L")
    vc_in["own"].wait_recv()
    z1.wait_recv()
    vs[:, :, zh] = (dv[:, :, zh, co].astype(jnp.float32) + vc[:, :, zh].astype(jnp.float32) + vz[...].astype(jnp.float32)).astype(vs.dtype)
    v1 = ship(vs.at[LOW, opp, zh], vxl, "R")
    v2 = ship(vs.at[HIGH, opp, zh], vxr, "L")
    kc_in["own"].wait_recv()
    k3.wait_recv()
    k4.wait_recv()
    ks[:, x] = (dk[:, x, :, co].astype(jnp.float32) + kc[:, x].astype(jnp.float32) + kl[...].astype(jnp.float32) + kr[...].astype(jnp.float32)).astype(ks.dtype)
    z2 = ship(ks.at[:, x, other], kz, "Z")
    v1.wait_recv()
    vs[LOW, right, zh] = add(vs[LOW, right, zh], vxl[...])
    v3 = ship(vs.at[:, right, zh], vl, "R")
    v2.wait_recv()
    vs[HIGH, left, zh] = add(vs[HIGH, left, zh], vxr[...])
    v4 = ship(vs.at[:, left, zh], vr, "L")
    last = []

    def spread(total, buf, a):
        for d in range(1, 8):
            q = (p + d) % 8
            cp = links.make(total.at[q], buf.at[:, pl.ds(pl.multiple_of(p * D, D), D)], (q, c))
            cp.start()
            last.append(cp)
        cp = pltpu.make_async_copy(total.at[p], buf.at[:, pl.ds(pl.multiple_of(p * D, D), D)], own_sem.at[a])
        cp.start()
        return cp

    z2.wait_recv()
    kz[...] = add(ks[:, x, zh], kz[...])
    own_k = spread(kz, okb, 0)
    v3.wait_recv()
    v4.wait_recv()
    vl[...] = (vs[:, x, zh].astype(jnp.float32) + vl[...].astype(jnp.float32) + vr[...].astype(jnp.float32)).astype(vs.dtype)
    own_v = spread(vl, ovb, 1)
    own_k.wait()
    own_v.wait()
    for cp in last:
        cp.wait_recv()
    ok[...] = okb[...]
    ov[...] = ovb[...]
    for cp in sent + last:
        cp.wait_send()


def reduce(dk, dv):
    rows = dk.shape[0] // 128
    bf = dk.dtype
    vm = lambda *s: pltpu.VMEM(s + (rows, D), bf)
    shape = (8, 4, 2, 2, rows, D)
    vmem = pl.BlockSpec(memory_space=pltpu.VMEM)
    out = jax.ShapeDtypeStruct((rows, 8 * D), bf)
    n = 48
    return pl.pallas_call(
        reduce_kernel,
        out_shape=(out, out),
        in_specs=[vmem] * 2,
        out_specs=[vmem] * 2,
        scratch_shapes=[vm(8, 4, 2), vm(8, 4, 2), vm(8, 4, 2), vm(8, 4, 2), vm(4, 2), vm(4, 2), vm(8, 2), vm(8, 2), vm(8), vm(8, 4),
                        vm(4), vm(4), vm(8), vm(8), pltpu.VMEM((rows, 8 * D), bf), pltpu.VMEM((rows, 8 * D), bf),
                        pltpu.SemaphoreType.DMA((n,)), pltpu.SemaphoreType.DMA((n,)), pltpu.SemaphoreType.DMA((2,))],
        compiler_params=pltpu.CompilerParams(collective_id=1, has_side_effects=True, vmem_limit_bytes=48 << 20),
    )(dk.reshape(shape), dv.reshape(shape))


KC = 256
RB = 64
NEG = -1e30


def fold8(x, op):
    return op(x.reshape(x.shape[0] // 8, 8, x.shape[1]), axis=0)


def attn_kernel(assign, lengths, offsets, q, do, ck, cv, k, v,
                dq, dck, dcv, dk, dv, slots, s_ref, dp_ref, dka, dva, dcka, dcva):
    device = lax.axis_index("cand")
    rows = q.shape[0]
    heads = q.shape[1] // D
    plen = k.shape[0]
    lanes = heads * RB
    scale = 1.0 / math.sqrt(D)
    c2 = scale * math.log2(math.e)

    def place(i, carry):
        slot, start = carry
        slots[0, slot] = start
        slots[1, slot] = start + lengths[i]
        slots[2, slot] = offsets[i]
        hit = assign[i] == device
        return (jnp.where(hit, slot + 1, slot), jnp.where(hit, start + lengths[i], start))

    lax.fori_loop(0, assign.shape[0], place, (jnp.int32(0), jnp.int32(0)))
    dka[...] = jnp.zeros_like(dka)
    dva[...] = jnp.zeros_like(dva)
    dcka[...] = jnp.zeros_like(dcka)
    dcva[...] = jnp.zeros_like(dcva)

    @pl.loop(0, rows // RB)
    def _(b):
        r0 = pl.multiple_of(b * RB, RB)
        row = r0 + (lax.broadcasted_iota(jnp.int32, (1, lanes), 1) & (RB - 1))
        off = jnp.zeros((1, lanes), jnp.int32)
        first = jnp.zeros((1, lanes), jnp.int32) + rows
        max_off = jnp.int32(0)
        min_off = jnp.int32(plen)
        for i in range(4):
            lo, hi, o = slots[0, i], slots[1, i], slots[2, i]
            inside = (row >= lo) & (row < hi)
            off = jnp.where(inside, o, off)
            first = jnp.where(inside, lo, first)
            meets = (lo < r0 + RB) & (hi > r0)
            max_off = jnp.maximum(max_off, jnp.where(meets, o, 0))
            min_off = jnp.minimum(min_off, jnp.where(meets, o, plen))
        valid = off > 0
        n_all = (max_off + KC - 1) // KC
        n_free = jnp.minimum(min_off // KC, n_all)
        off = jnp.where(valid, off, plen)

        qb = jnp.concatenate([q[pl.ds(r0, RB), h * D:(h + 1) * D] for h in range(heads)], axis=0)
        db = jnp.concatenate([do[pl.ds(r0, RB), h * D:(h + 1) * D] for h in range(heads)], axis=0)

        @pl.when(max_off == 0)
        def _():
            dq[pl.ds(r0, RB), :] = jnp.zeros((RB, heads * D), dq.dtype)

        @pl.when(max_off > 0)
        def _():
            nt = (((1,), (1,)), ((), ()))
            w0 = pl.multiple_of(jnp.maximum(r0 - RB, 0), RB)

            def score(kk, vv, at, mask, m):
                n = kk.shape[0]
                s = lax.dot_general(kk, qb, nt, preferred_element_type=jnp.float32)
                if mask is not None:
                    s = jnp.where(mask, s, NEG)
                s_ref[pl.ds(at, n), :] = s
                dp_ref[pl.ds(at, n), :] = lax.dot_general(vv, db, nt, preferred_element_type=jnp.float32)
                return jnp.maximum(m, fold8(s, jnp.max))

            def free(c, m):
                at = pl.multiple_of(c * KC, KC)
                return score(k[pl.ds(at, KC), :], v[pl.ds(at, KC), :], at, None, m)

            def masked(c, m):
                at = pl.multiple_of(c * KC, KC)
                key = at + lax.broadcasted_iota(jnp.int32, (KC, lanes), 0)
                return score(k[pl.ds(at, KC), :], v[pl.ds(at, KC), :], at, key < off, m)

            m = jnp.full((8, lanes), NEG, jnp.float32)
            m = lax.fori_loop(0, n_free, free, m)
            m = lax.fori_loop(n_free, n_all, masked, m)
            key = w0 + lax.broadcasted_iota(jnp.int32, (2 * RB, lanes), 0)
            m = score(ck[pl.ds(w0, 2 * RB), :], cv[pl.ds(w0, 2 * RB), :], plen,
                      (key >= first) & (key <= row), m)
            mc = jnp.max(m, axis=0, keepdims=True) * c2

            def expo(at, n, carry):
                l, d = carry
                e = jnp.exp2(s_ref[pl.ds(at, n), :] * c2 - mc)
                s_ref[pl.ds(at, n), :] = e
                return (l + fold8(e, jnp.sum), d + fold8(e * dp_ref[pl.ds(at, n), :], jnp.sum))

            zero = jnp.zeros((8, lanes), jnp.float32)
            carry = lax.fori_loop(0, n_all, lambda c, x: expo(pl.multiple_of(c * KC, KC), KC, x), (zero, zero))
            l, d = expo(plen, 2 * RB, carry)
            l = jnp.sum(l, axis=0, keepdims=True)
            inv = jnp.where(valid, 1.0 / l, 0.0)
            delta = jnp.sum(d, axis=0, keepdims=True) * inv

            def grads(at, n, kk):
                p = s_ref[pl.ds(at, n), :] * inv
                ds = (p * (dp_ref[pl.ds(at, n), :] - delta)).astype(jnp.bfloat16)
                p = p.astype(jnp.bfloat16)
                gv = jnp.dot(p, db, preferred_element_type=jnp.float32)
                gk = jnp.dot(ds, qb, preferred_element_type=jnp.float32)
                gq = lax.dot_general(kk, ds, (((0,), (0,)), ((), ())), preferred_element_type=jnp.float32)
                return gk, gv, gq

            def back(c, gq):
                at = pl.multiple_of(c * KC, KC)
                gk, gv, g = grads(at, KC, k[pl.ds(at, KC), :])
                dka[pl.ds(at, KC), :] += gk
                dva[pl.ds(at, KC), :] += gv
                return gq + g

            gq = lax.fori_loop(0, n_all, back, jnp.zeros((D, lanes), jnp.float32))
            gk, gv, g = grads(plen, 2 * RB, ck[pl.ds(w0, 2 * RB), :])
            dcka[pl.ds(w0, 2 * RB), :] += gk
            dcva[pl.ds(w0, 2 * RB), :] += gv
            gq = ((gq + g) * scale).T.astype(dq.dtype)
            for h in range(heads):
                dq[pl.ds(r0, RB), h * D:(h + 1) * D] = gq[h * RB:(h + 1) * RB, :]

    dk[...] = (dka[...] * scale).astype(dk.dtype)
    dv[...] = dva[...].astype(dv.dtype)
    dck[...] = (dcka[...] * scale).astype(dck.dtype)
    dcv[...] = dcva[...].astype(dcv.dtype)


def attn(assign, lengths, offsets, q, do, ck, cv, k, v):
    rows, width = q.shape
    plen = k.shape[0]
    lanes = width // D * RB
    bf = jnp.bfloat16
    smem = pl.BlockSpec(memory_space=pltpu.SMEM)
    vmem = pl.BlockSpec(memory_space=pltpu.VMEM)
    f32 = jnp.float32
    return pl.pallas_call(
        attn_kernel,
        out_shape=(
            jax.ShapeDtypeStruct((rows, width), bf),
            jax.ShapeDtypeStruct((rows, D), bf),
            jax.ShapeDtypeStruct((rows, D), bf),
            jax.ShapeDtypeStruct((plen, D), bf),
            jax.ShapeDtypeStruct((plen, D), bf),
        ),
        in_specs=[smem] * 3 + [vmem] * 6,
        out_specs=[vmem] * 5,
        scratch_shapes=[
            pltpu.SMEM((3, 8), jnp.int32),
            pltpu.VMEM((plen + 2 * RB, lanes), f32),
            pltpu.VMEM((plen + 2 * RB, lanes), f32),
            pltpu.VMEM((plen, D), f32),
            pltpu.VMEM((plen, D), f32),
            pltpu.VMEM((rows, D), f32),
            pltpu.VMEM((rows, D), f32),
        ],
        compiler_params=pltpu.CompilerParams(vmem_limit_bytes=60 << 20),
    )(assign, lengths, offsets, q, do, ck, cv, k, v)


def per_device(query, grad_out, continuation_key, continuation_value, prompt_key, shared_prompt_value, assign, lengths, offsets):
    keys, values = gather(prompt_key, shared_prompt_value)
    query_grad, key_grad, value_grad, dk, dv = attn(
        assign, lengths, offsets, query, grad_out, continuation_key, continuation_value, keys, values
    )
    prompt_key_grad, prompt_value_grad = reduce(dk, dv)
    return query_grad, key_grad, value_grad, prompt_key_grad, prompt_value_grad


def solution(mesh):
    rows = P("cand", "prefix")
    owned = P(("prefix", "cand"), None)
    return jax.shard_map(
        per_device,
        mesh=mesh,
        in_specs=(rows, rows, rows, rows, owned, owned, P(), P(), P()),
        out_specs=(rows, rows, rows, owned, owned),
        check_vma=False,
    )
```

```python
import functools
import math

import jax
import jax.numpy as jnp
from jax import lax
from jax.experimental import pallas as pl
from jax.experimental.pallas import tpu as pltpu
from jax.sharding import PartitionSpec as P

D = 128
MESH = pl.DeviceIdType.MESH
ALL = pl.ds(0, 8)
HEADS_FAR = [(2, 1), (2, 0), (1, 1), (3, 1), (1, 0), (3, 0), (0, 1), (0, 0)]
GROUPS = [
    [(2, dz, dy, dl) for dz in (1, 0) for dy, dl in HEADS_FAR],
    [(1, dz, dy, dl) for dz in (1, 0) for dy, dl in HEADS_FAR],
    [(3, dz, dy, dl) for dz in (1, 0) for dy, dl in HEADS_FAR],
    [(0, 1, dy, dl) for dy, dl in HEADS_FAR],
    [(0, 0, dy, dl) for dy, dl in HEADS_FAR[:-1]],
]


class Place:
    def __init__(self):
        self.p, self.c = lax.axis_index("prefix"), lax.axis_index("cand")
        self.x, self.zh, self.co = self.c // 4, (self.c // 2) % 2, self.c % 2
        self.zl, self.y = self.p // 4, self.p % 4
        self.partner = (self.p, self.c + 1 - 2 * self.co)

    def head(self, dy, dl):
        return ((self.zl + dl) % 2) * 4 + (self.y + dy) % 4

    def chip(self, dx, dz):
        return (self.x + dx) % 4, (self.zh + dz) % 2

    def peer(self, dx, dz, dy, dl):
        x, zh = self.chip(dx, dz)
        return (self.head(dy, dl), x * 4 + zh * 2 + self.co)


def greet(at):
    barrier = pltpu.get_barrier_semaphore()
    n = 1
    pl.semaphore_signal(barrier, inc=1, device_id=at.partner, device_id_type=MESH)
    for group in GROUPS:
        for offset in group:
            n += 1
            pl.semaphore_signal(barrier, inc=1, device_id=at.peer(*offset), device_id_type=MESH)
    pl.semaphore_wait(barrier, n)


def remote(src, dst, send, recv, peer):
    return pltpu.make_async_remote_copy(src_ref=src, dst_ref=dst, send_sem=send, recv_sem=recv, device_id=peer, device_id_type=MESH)


def columns(head):
    return pl.ds(pl.multiple_of(head * D, D), D)


def gather_kernel(pk, pv, fk, fv, send, recv, send_near, recv_near, send_core, recv_core, own_sem):
    at = Place()
    greet(at)
    pairs = ((pk, fk), (pv, fv))
    near = []
    for g, group in enumerate(GROUPS):
        for a, (src, dst) in enumerate(pairs):
            for i, offset in enumerate(group):
                peer = at.peer(*offset)
                s, r = (send.at[a, g], recv.at[a, g]) if g < 4 else (send_near.at[a, i], recv_near.at[a, i])
                cp = remote(src.at[:, columns(peer[0])], dst.at[at.p, at.x, at.zh, at.co], s, r, peer)
                cp.start()
                if g == 4:
                    near.append(cp)
    own = []
    for a, (src, dst) in enumerate(pairs):
        cp = pltpu.make_async_copy(src.at[:, columns(at.p)], dst.at[at.p, at.x, at.zh, at.co], own_sem.at[a])
        cp.start()
        own.append(cp)
    regions = [(at.chip(2, 0)[0], pl.ds(0, 2)), (at.chip(3, 0)[0], pl.ds(0, 2)), (at.chip(1, 0)[0], pl.ds(0, 2)), (at.x, 1 - at.zh), (at.x, at.zh)]
    handed = []

    def hand(a, g):
        ref = pairs[a][1].at[ALL, regions[g][0], regions[g][1], at.co]
        cp = remote(ref, ref, send_core.at[a, g], recv_core.at[a, g], at.partner)
        cp.start()
        handed.append(cp)

    for cp in near:
        cp.wait_recv()
    for cp in own:
        cp.wait()
    hand(0, 4)
    hand(1, 4)
    bulk = []
    for g in range(4):
        for a in range(2):
            ref = pairs[a][1].at[ALL, regions[g][0], regions[g][1], at.co]
            cp = remote(ref, ref, send.at[a, g], recv.at[a, g], at.partner)
            cp.wait_recv()
            bulk.append(cp)
            hand(a, g)
    for cp in handed:
        cp.wait_recv()
    for cp in bulk + near + handed:
        cp.wait_send()


def gather(pk, pv):
    rows = pk.shape[0]
    out = jax.ShapeDtypeStruct((8, 4, 2, 2, rows, D), pk.dtype)
    anyspace = pl.BlockSpec(memory_space=pl.ANY)
    dma = lambda *s: pltpu.SemaphoreType.DMA(s)
    fk, fv = pl.pallas_call(
        gather_kernel,
        out_shape=(out, out),
        in_specs=[anyspace] * 2,
        out_specs=[anyspace] * 2,
        scratch_shapes=[dma(2, 4), dma(2, 4), dma(2, 7), dma(2, 7), dma(2, 5), dma(2, 5), dma(2)],
        compiler_params=pltpu.CompilerParams(collective_id=0, has_side_effects=True),
    )(pk, pv)
    return fk.reshape(-1, D), fv.reshape(-1, D)


def reduce_kernel(dk, dv, ok, ov, mine, other, part, came, send, recv, send_near, recv_near, send_core, recv_core, own_sem):
    at = Place()
    f32 = jnp.float32
    order = [at.chip(2, 0)[0], at.chip(1, 0)[0], at.chip(3, 0)[0], at.x]
    loads = []
    for i, x in enumerate(order):
        for a, src in enumerate((dk, dv)):
            cp = pltpu.make_async_copy(src.at[:, x, :, at.co], mine.at[a, i], own_sem.at[a, i])
            cp.start()
            loads.append(cp)
    greet(at)
    crossed = []
    for i, x in enumerate(order):
        for a, src in enumerate((dk, dv)):
            cp = remote(src.at[:, x, :, 1 - at.co], other.at[a, i], send_core.at[a, i], recv_core.at[a, i], at.partner)
            cp.start()
            crossed.append(cp)
    near = []
    slot = at.x * 2 + at.zh
    for i in range(4):
        for a in range(2):
            loads[2 * i + a].wait()
            crossed[2 * i + a].wait_recv()
            part[a, i] = (mine[a, i].astype(f32) + other[a, i].astype(f32)).astype(part.dtype)
            for g in ((i,) if i < 3 else (3, 4)):
                for j, offset in enumerate(GROUPS[g]):
                    peer = at.peer(*offset)
                    s, r = (send.at[a, g], recv.at[a, g]) if g < 4 else (send_near.at[a, j], recv_near.at[a, j])
                    zh = at.chip(0, offset[1])[1]
                    cp = remote(part.at[a, i, peer[0], zh], came.at[a, slot, :, columns(at.p)], s, r, peer)
                    cp.start()
                    if g == 4:
                        near.append(cp)
    own = []
    for a in range(2):
        cp = pltpu.make_async_copy(part.at[a, 3, at.p, at.zh], came.at[a, slot, :, columns(at.p)], own_sem.at[a, 4])
        cp.start()
        own.append(cp)
    bulk = []
    for g in range(4):
        for a in range(2):
            ref = mine.at[a, g] if g < 3 else mine.at[a, g, :, 0]
            cp = remote(ref, ref, send.at[a, g], recv.at[a, g], at.partner)
            cp.wait_recv()
            bulk.append(cp)
    for cp in near:
        cp.wait_recv()
    for cp in own:
        cp.wait()
    for a, out in enumerate((ok, ov)):
        total = came[a, 0].astype(f32)
        for s in range(1, 8):
            total += came[a, s].astype(f32)
        out[...] = total.astype(out.dtype)
    for cp in crossed + bulk + near:
        cp.wait_send()


def reduce(dk, dv):
    rows = dk.shape[0] // 128
    bf = dk.dtype
    shape = (8, 4, 2, 2, rows, D)
    out = jax.ShapeDtypeStruct((rows, 8 * D), bf)
    dma = lambda *s: pltpu.SemaphoreType.DMA(s)
    buf = pltpu.VMEM((2, 4, 8, 2, rows, D), bf)
    return pl.pallas_call(
        reduce_kernel,
        out_shape=(out, out),
        in_specs=[pl.BlockSpec(memory_space=pl.ANY)] * 2,
        out_specs=[pl.BlockSpec(memory_space=pltpu.VMEM)] * 2,
        scratch_shapes=[buf, buf, buf, pltpu.VMEM((2, 8, rows, 8 * D), bf),
                        dma(2, 4), dma(2, 4), dma(2, 7), dma(2, 7), dma(2, 4), dma(2, 4), dma(2, 5)],
        compiler_params=pltpu.CompilerParams(collective_id=1, has_side_effects=True, vmem_limit_bytes=48 << 20),
    )(dk.reshape(shape), dv.reshape(shape))


KC = 512
RB = 64
NEG = -1e30
NT = (((1,), (1,)), ((), ()))
TN = (((0,), (0,)), ((), ()))
F32 = jnp.float32


def groups(x):
    return x.reshape(x.shape[0] // 8, 8, x.shape[1])


def attn_kernel(assign, lengths, offsets, q, do, ck, cv, k, v,
                dq, dck, dcv, dk, dv, slots, e_ref, dp_ref, mx_ref, dkt, dvt, dcka, dcva, t_ref, p_ref, ds_ref, gq_ref, kt_ref):
    owners, rows, width = q.shape
    heads = width // D
    plen = k.shape[0]
    lanes = heads * RB
    per_owner = rows // RB
    scale = 1.0 / math.sqrt(D)
    cand = lax.axis_index("cand")
    base = cand - lax.rem(cand, owners)

    for o in range(owners):
        def place_rows(i, carry):
            slot, start = carry
            slots[o, 0, slot] = start
            slots[o, 1, slot] = start + lengths[i]
            slots[o, 2, slot] = offsets[i]
            hit = assign[i] == base + o
            return (jnp.where(hit, slot + 1, slot), jnp.where(hit, start + lengths[i], start))

        lax.fori_loop(0, assign.shape[0], place_rows, (jnp.int32(0), jnp.int32(0)))
    @pl.loop(0, plen // KC)
    def _(c):
        at = pl.multiple_of(c * KC, KC)
        kt_ref[:, pl.ds(at, KC)] = k[pl.ds(at, KC), :].T

    dkt[...] = jnp.zeros_like(dkt)
    dvt[...] = jnp.zeros_like(dvt)
    dcka[...] = jnp.zeros_like(dcka)
    dcva[...] = jnp.zeros_like(dcva)

    @pl.loop(0, owners * per_owner)
    def _(step):
        o = step // per_owner
        r0 = pl.multiple_of((step % per_owner) * RB, RB)
        row = r0 + (lax.broadcasted_iota(jnp.int32, (1, lanes), 1) & (RB - 1))
        off = jnp.zeros((1, lanes), jnp.int32)
        first = jnp.zeros((1, lanes), jnp.int32) + rows
        max_off = jnp.int32(0)
        min_off = jnp.int32(plen)
        for i in range(4):
            lo, hi, n = slots[o, 0, i], slots[o, 1, i], slots[o, 2, i]
            inside = (row >= lo) & (row < hi)
            off = jnp.where(inside, n, off)
            first = jnp.where(inside, lo, first)
            meets = (lo < r0 + RB) & (hi > r0)
            max_off = jnp.maximum(max_off, jnp.where(meets, n, 0))
            min_off = jnp.minimum(min_off, jnp.where(meets, n, plen))
        valid = off > 0
        n_all = (max_off + KC - 1) // KC
        n_free = jnp.minimum(min_off // KC, n_all)
        off = jnp.where(valid, off, plen)

        @pl.when(max_off == 0)
        def _():
            dq[o, pl.ds(r0, RB), :] = jnp.zeros((RB, width), dq.dtype)

        @pl.when(max_off > 0)
        def _():
            qb = jnp.concatenate([q[o, pl.ds(r0, RB), h * D:(h + 1) * D] for h in range(heads)], axis=0)
            db = jnp.concatenate([do[o, pl.ds(r0, RB), h * D:(h + 1) * D] for h in range(heads)], axis=0)
            qt, dt = qb.T, db.T
            w0 = pl.multiple_of(jnp.maximum(r0 - RB, 0), RB)

            def raw(kk, mask):
                t = lax.dot_general(kk, qb, NT, preferred_element_type=F32) * scale
                return t if mask is None else jnp.where(mask, t, NEG)

            def weigh(vv, at, slot, n, old, m, l, d):
                e = jnp.exp(groups(t_ref[pl.ds(0, n), :]) - m[None])
                mx_ref[slot] = m
                e_ref[pl.ds(at, n), :] = e.reshape(n, lanes).astype(jnp.bfloat16)
                dp = lax.dot_general(vv, db, NT, preferred_element_type=F32)
                dp_ref[pl.ds(at, n), :] = dp
                fade = jnp.exp(old - m)
                return l * fade + jnp.sum(e, axis=0), d * fade + jnp.sum(e * groups(dp), axis=0)

            def mask_at(at):
                return at + lax.broadcasted_iota(jnp.int32, (KC, lanes), 0) < off

            def piece(ref, c):
                return ref[pl.ds(pl.multiple_of(c * KC, KC), KC), :]

            def step_to(c, mask, carry):
                old, m, l, d = carry
                t = raw(piece(k, c), mask)
                l, d = weigh(piece(v, c - 1), pl.multiple_of((c - 1) * KC, KC), c - 1, KC, old, m, l, d)
                t_ref[...] = t
                return m, jnp.maximum(m, jnp.max(groups(t), axis=0)), l, d

            zero = jnp.zeros((8, lanes), F32)
            low = jnp.full((8, lanes), NEG, F32)
            near = pl.ds(w0, 2 * RB)
            last = plen // KC
            key = w0 + lax.broadcasted_iota(jnp.int32, (2 * RB, lanes), 0)
            first_t = raw(ck[o, near, :], (key >= first) & (key <= row))
            m = jnp.max(groups(first_t), axis=0)
            t_ref[pl.ds(0, 2 * RB), :] = first_t
            t = raw(piece(k, 0), None)
            l, d = weigh(cv[o, near, :], plen, last, 2 * RB, low, m, zero, zero)
            t_ref[...] = t
            carry = (m, jnp.maximum(m, jnp.max(groups(t), axis=0)), l, d)
            turn = jnp.maximum(n_free, 1)
            carry = lax.fori_loop(1, turn, lambda c, x: step_to(c, None, x), carry)
            carry = lax.fori_loop(turn, n_all, lambda c, x: step_to(c, mask_at(c * KC), x), carry)
            old, m, l, d = carry
            l, d = weigh(piece(v, n_all - 1), pl.multiple_of((n_all - 1) * KC, KC), n_all - 1, KC, old, m, l, d)

            top = jnp.max(m, axis=0, keepdims=True)
            fade = jnp.exp(m - top)
            inv = jnp.where(valid, 1.0 / jnp.sum(l * fade, axis=0, keepdims=True), 0.0)
            delta = jnp.sum(d * fade, axis=0, keepdims=True) * inv
            delta = jnp.broadcast_to(delta, (8, lanes))

            def grads(at, n, slot):
                g = (jnp.exp(mx_ref[slot] - top) * inv).astype(jnp.bfloat16)
                g = jnp.concatenate([g, g], axis=0)
                p = (e_ref[pl.ds(at, n), :].reshape(n // 16, 16, lanes) * g[None]).reshape(n, lanes)
                u = groups(dp_ref[pl.ds(at, n), :]) - delta[None]
                return p, p * u.reshape(n, lanes).astype(jnp.bfloat16)

            def products(c):
                at = pl.multiple_of(c * KC, KC)
                p, ds = p_ref[...], ds_ref[...]
                dvt[:, pl.ds(at, KC)] += lax.dot_general(dt, p, NT, preferred_element_type=F32)
                dkt[:, pl.ds(at, KC)] += lax.dot_general(qt, ds, NT, preferred_element_type=F32)
                gq_ref[...] += jnp.dot(kt_ref[:, pl.ds(at, KC)], ds, preferred_element_type=F32)

            def back(c, carry):
                products(c - 1)
                p_ref[...], ds_ref[...] = grads(pl.multiple_of(c * KC, KC), KC, c)
                return carry

            p, ds = grads(plen, 2 * RB, last)
            p_ref[...], ds_ref[...] = grads(0, KC, 0)
            dcva[o, near, :] += jnp.dot(p, db, preferred_element_type=F32)
            dcka[o, near, :] += jnp.dot(ds, qb, preferred_element_type=F32)
            gq_ref[...] = lax.dot_general(ck[o, near, :], ds, TN, preferred_element_type=F32)
            lax.fori_loop(1, n_all, back, 0)
            products(n_all - 1)
            gq = (gq_ref[...] * scale).T.astype(dq.dtype)
            for h in range(heads):
                dq[o, pl.ds(r0, RB), h * D:(h + 1) * D] = gq[h * RB:(h + 1) * RB, :]

    @pl.loop(0, plen // KC)
    def _(c):
        at = pl.multiple_of(c * KC, KC)
        dk[pl.ds(at, KC), :] = (dkt[:, pl.ds(at, KC)] * scale).T.astype(dk.dtype)
        dv[pl.ds(at, KC), :] = dvt[:, pl.ds(at, KC)].T.astype(dv.dtype)

    dck[...] = (dcka[...] * scale).astype(dck.dtype)
    dcv[...] = dcva[...].astype(dcv.dtype)


def attn_call(assign, lengths, offsets, q, do, ck, cv, k, v):
    owners, rows, width = q.shape
    plen = k.shape[0]
    lanes = width // D * RB
    bf = jnp.bfloat16
    smem = pl.BlockSpec(memory_space=pltpu.SMEM)
    vmem = pl.BlockSpec(memory_space=pltpu.VMEM)
    return pl.pallas_call(
        attn_kernel,
        out_shape=(
            jax.ShapeDtypeStruct((owners, rows, width), bf),
            jax.ShapeDtypeStruct((owners, rows, D), bf),
            jax.ShapeDtypeStruct((owners, rows, D), bf),
            jax.ShapeDtypeStruct((plen, D), bf),
            jax.ShapeDtypeStruct((plen, D), bf),
        ),
        in_specs=[smem] * 3 + [vmem] * 6,
        out_specs=[vmem] * 5,
        scratch_shapes=[
            pltpu.SMEM((owners, 3, 8), jnp.int32),
            pltpu.VMEM((plen + 2 * RB, lanes), bf),
            pltpu.VMEM((plen + 2 * RB, lanes), F32),
            pltpu.VMEM((plen // KC + 1, 8, lanes), F32),
            pltpu.VMEM((D, plen), F32),
            pltpu.VMEM((D, plen), F32),
            pltpu.VMEM((owners, rows, D), F32),
            pltpu.VMEM((owners, rows, D), F32),
            pltpu.VMEM((KC, lanes), F32),
            pltpu.VMEM((KC, lanes), bf),
            pltpu.VMEM((KC, lanes), bf),
            pltpu.VMEM((D, lanes), F32),
            pltpu.VMEM((D, plen), bf),
        ],
        compiler_params=pltpu.CompilerParams(vmem_limit_bytes=56 << 20),
    )(assign, lengths, offsets, q, do, ck, cv, k, v)


def attn(assign, lengths, offsets, q, do, ck, cv, k, v):
    dq, dck, dcv, dk, dv = attn_call(assign, lengths, offsets, q[None], do[None], ck[None], cv[None], k, v)
    return dq[0], dck[0], dcv[0], dk, dv


def per_device(query, grad_out, continuation_key, continuation_value, prompt_key, shared_prompt_value, assign, lengths, offsets):
    keys, values = gather(prompt_key, shared_prompt_value)
    query_grad, key_grad, value_grad, dk, dv = attn(
        assign, lengths, offsets, query, grad_out, continuation_key, continuation_value, keys, values
    )
    prompt_key_grad, prompt_value_grad = reduce(dk, dv)
    return query_grad, key_grad, value_grad, prompt_key_grad, prompt_value_grad


def solution(mesh):
    rows = P("cand", "prefix")
    owned = P(("prefix", "cand"), None)
    return jax.shard_map(
        per_device,
        mesh=mesh,
        in_specs=(rows, rows, rows, rows, owned, owned, P(), P(), P()),
        out_specs=(rows, rows, rows, owned, owned),
        check_vma=False,
    )
```

```python
import functools
import math

import jax
import jax.numpy as jnp
from jax import lax
from jax.experimental import pallas as pl
from jax.experimental.pallas import tpu as pltpu
from jax.sharding import PartitionSpec as P

D = 128
MESH = pl.DeviceIdType.MESH
ALL = pl.ds(0, 8)
HEADS_FAR = [(2, 1), (2, 0), (1, 1), (3, 1), (1, 0), (3, 0), (0, 1), (0, 0)]
GROUPS = [
    [(2, dz, dy, dl) for dz in (1, 0) for dy, dl in HEADS_FAR],
    [(1, dz, dy, dl) for dz in (1, 0) for dy, dl in HEADS_FAR],
    [(3, dz, dy, dl) for dz in (1, 0) for dy, dl in HEADS_FAR],
    [(0, 1, dy, dl) for dy, dl in HEADS_FAR],
    [(0, 0, dy, dl) for dy, dl in HEADS_FAR[:-1]],
]


class Place:
    def __init__(self):
        self.p, self.c = lax.axis_index("prefix"), lax.axis_index("cand")
        self.x, self.zh, self.co = self.c // 4, (self.c // 2) % 2, self.c % 2
        self.zl, self.y = self.p // 4, self.p % 4
        self.partner = (self.p, self.c + 1 - 2 * self.co)

    def head(self, dy, dl):
        return ((self.zl + dl) % 2) * 4 + (self.y + dy) % 4

    def chip(self, dx, dz):
        return (self.x + dx) % 4, (self.zh + dz) % 2

    def peer(self, dx, dz, dy, dl):
        x, zh = self.chip(dx, dz)
        return (self.head(dy, dl), x * 4 + zh * 2 + self.co)


def greet(at):
    barrier = pltpu.get_barrier_semaphore()
    n = 1
    pl.semaphore_signal(barrier, inc=1, device_id=at.partner, device_id_type=MESH)
    for group in GROUPS:
        for offset in group:
            n += 1
            pl.semaphore_signal(barrier, inc=1, device_id=at.peer(*offset), device_id_type=MESH)
    pl.semaphore_wait(barrier, n)


def remote(src, dst, send, recv, peer):
    return pltpu.make_async_remote_copy(src_ref=src, dst_ref=dst, send_sem=send, recv_sem=recv, device_id=peer, device_id_type=MESH)


def columns(head):
    return pl.ds(pl.multiple_of(head * D, D), D)


def gather_kernel(pk, pv, full, stage, send, recv, send_near, recv_near, send_core, recv_core, own_sem):
    at = Place()
    staged = []
    for a, src in enumerate((pk, pv)):
        cp = pltpu.make_async_copy(src, stage.at[a], own_sem.at[a])
        cp.start()
        staged.append(cp)
    greet(at)
    for cp in staged:
        cp.wait()
    near = []
    for g, group in enumerate(GROUPS):
        for i, offset in enumerate(group):
            peer = at.peer(*offset)
            s, r = (send.at[g], recv.at[g]) if g < 4 else (send_near.at[i], recv_near.at[i])
            cp = remote(stage.at[:, :, columns(peer[0])], full.at[:, at.p, at.x, at.zh, at.co], s, r, peer)
            cp.start()
            if g == 4:
                near.append(cp)
    own = pltpu.make_async_copy(stage.at[:, :, columns(at.p)], full.at[:, at.p, at.x, at.zh, at.co], own_sem.at[2])
    own.start()
    regions = [(at.chip(2, 0)[0], pl.ds(0, 2)), (at.chip(3, 0)[0], pl.ds(0, 2)), (at.chip(1, 0)[0], pl.ds(0, 2)), (at.x, 1 - at.zh), (at.x, at.zh)]
    handed = []

    def hand(g):
        ref = full.at[:, ALL, regions[g][0], regions[g][1], at.co]
        cp = remote(ref, ref, send_core.at[g], recv_core.at[g], at.partner)
        cp.start()
        handed.append(cp)

    bulk = []
    for g in range(4):
        ref = full.at[:, ALL, regions[g][0], regions[g][1], at.co]
        cp = remote(ref, ref, send.at[g], recv.at[g], at.partner)
        cp.wait_recv()
        bulk.append(cp)
        hand(g)
    for cp in near:
        cp.wait_recv()
    own.wait()
    hand(4)
    for cp in handed:
        cp.wait_recv()
    for cp in bulk + near + handed:
        cp.wait_send()


def gather(pk, pv):
    rows = pk.shape[0]
    hbm = pl.BlockSpec(memory_space=pltpu.HBM)
    dma = lambda *s: pltpu.SemaphoreType.DMA(s)
    full = pl.pallas_call(
        gather_kernel,
        out_shape=jax.ShapeDtypeStruct((2, 8, 4, 2, 2, rows, D), pk.dtype),
        in_specs=[hbm] * 2,
        out_specs=hbm,
        scratch_shapes=[pltpu.VMEM((2, rows, 8 * D), pk.dtype), dma(4), dma(4), dma(7), dma(7), dma(5), dma(5), dma(3)],
        compiler_params=pltpu.CompilerParams(collective_id=0, has_side_effects=True),
    )(pk, pv)
    return full.reshape(2, -1, D)


def reduce_kernel(dk, dv, ok, ov, mine, other, part, came, send, recv, send_near, recv_near, send_core, recv_core, own_sem):
    at = Place()
    f32 = jnp.float32
    order = [at.chip(2, 0)[0], at.chip(1, 0)[0], at.chip(3, 0)[0], at.x]
    loads = []
    for i, x in enumerate(order):
        for a, src in enumerate((dk, dv)):
            cp = pltpu.make_async_copy(src.at[:, x, :, at.co], mine.at[a, i], own_sem.at[a, i])
            cp.start()
            loads.append(cp)
    greet(at)
    crossed = []
    for i, x in enumerate(order):
        for a, src in enumerate((dk, dv)):
            cp = remote(src.at[:, x, :, 1 - at.co], other.at[a, i], send_core.at[a, i], recv_core.at[a, i], at.partner)
            cp.start()
            crossed.append(cp)
    near = []
    slot = at.x * 2 + at.zh
    for i in range(4):
        for a in range(2):
            loads[2 * i + a].wait()
            crossed[2 * i + a].wait_recv()
            part[a, i] = (mine[a, i].astype(f32) + other[a, i].astype(f32)).astype(part.dtype)
            for g in ((i,) if i < 3 else (3, 4)):
                for j, offset in enumerate(GROUPS[g]):
                    peer = at.peer(*offset)
                    s, r = (send.at[a, g], recv.at[a, g]) if g < 4 else (send_near.at[a, j], recv_near.at[a, j])
                    zh = at.chip(0, offset[1])[1]
                    cp = remote(part.at[a, i, peer[0], zh], came.at[a, slot, :, columns(at.p)], s, r, peer)
                    cp.start()
                    if g == 4:
                        near.append(cp)
    own = []
    for a in range(2):
        cp = pltpu.make_async_copy(part.at[a, 3, at.p, at.zh], came.at[a, slot, :, columns(at.p)], own_sem.at[a, 4])
        cp.start()
        own.append(cp)
    bulk = []
    for g in range(4):
        for a in range(2):
            ref = mine.at[a, g] if g < 3 else mine.at[a, g, :, 0]
            cp = remote(ref, ref, send.at[a, g], recv.at[a, g], at.partner)
            cp.wait_recv()
            bulk.append(cp)
    for cp in near:
        cp.wait_recv()
    for cp in own:
        cp.wait()
    for a, out in enumerate((ok, ov)):
        total = came[a, 0].astype(f32)
        for s in range(1, 8):
            total += came[a, s].astype(f32)
        out[...] = total.astype(out.dtype)
    for cp in crossed + bulk + near:
        cp.wait_send()


def reduce(dk, dv):
    rows = dk.shape[0] // 128
    bf = dk.dtype
    shape = (8, 4, 2, 2, rows, D)
    out = jax.ShapeDtypeStruct((rows, 8 * D), bf)
    dma = lambda *s: pltpu.SemaphoreType.DMA(s)
    buf = pltpu.VMEM((2, 4, 8, 2, rows, D), bf)
    return pl.pallas_call(
        reduce_kernel,
        out_shape=(out, out),
        in_specs=[pl.BlockSpec(memory_space=pltpu.HBM)] * 2,
        out_specs=[pl.BlockSpec(memory_space=pltpu.VMEM)] * 2,
        scratch_shapes=[buf, buf, buf, pltpu.VMEM((2, 8, rows, 8 * D), bf),
                        dma(2, 4), dma(2, 4), dma(2, 7), dma(2, 7), dma(2, 4), dma(2, 4), dma(2, 5)],
        compiler_params=pltpu.CompilerParams(collective_id=1, has_side_effects=True, vmem_limit_bytes=63 << 20),
    )(dk.reshape(shape), dv.reshape(shape))


KC = 512
RB = 64
NEG = -1e30
NT = (((1,), (1,)), ((), ()))
TN = (((0,), (0,)), ((), ()))
F32 = jnp.float32


def groups(x):
    return x.reshape(x.shape[0] // 8, 8, x.shape[1])


def attn_kernel(assign, lengths, offsets, q_in, do_in, ck_in, cv_in, kv, dq_out, dck_out, dcv_out, dk_out, dv_out,
                q, do, ck, cv, k, v, dq, dck, dcv, dk, dv, slots, e_ref, dp_ref, mx_ref, dkt, dvt, dcka, dcva,
                t_ref, p_ref, ds_ref, gq_ref, kt_ref, in_sem, dq_sem, out_sem):
    rows, width = q.shape
    heads = width // D
    plen = k.shape[0]
    lanes = heads * RB
    scale = 1.0 / math.sqrt(D)
    cand = lax.axis_index("cand")

    loads = [
        pltpu.make_async_copy(src, dst, in_sem.at[n])
        for n, (src, dst) in enumerate(((kv.at[0], k), (kv.at[1], v), (q_in, q), (do_in, do), (ck_in, ck), (cv_in, cv)))
    ]
    for cp in loads:
        cp.start()

    def place_rows(i, carry):
        slot, start = carry
        slots[0, slot] = start
        slots[1, slot] = start + lengths[i]
        slots[2, slot] = offsets[i]
        hit = assign[i] == cand
        return (jnp.where(hit, slot + 1, slot), jnp.where(hit, start + lengths[i], start))

    lax.fori_loop(0, assign.shape[0], place_rows, (jnp.int32(0), jnp.int32(0)), unroll=8)
    dkt[...] = jnp.zeros_like(dkt)
    dvt[...] = jnp.zeros_like(dvt)
    dcka[...] = jnp.zeros_like(dcka)
    dcva[...] = jnp.zeros_like(dcva)
    loads[0].wait()

    @pl.loop(0, plen // KC)
    def _(c):
        at = pl.multiple_of(c * KC, KC)
        kt_ref[:, pl.ds(at, KC)] = k[pl.ds(at, KC), :].T

    for cp in loads[1:]:
        cp.wait()

    def dq_copy(b):
        band = pl.ds(pl.multiple_of(b * RB, RB), RB)
        return pltpu.make_async_copy(dq.at[band, :], dq_out.at[band, :], dq_sem.at[b])

    @pl.loop(0, rows // RB)
    def _(b):
        r0 = pl.multiple_of(b * RB, RB)
        row = r0 + (lax.broadcasted_iota(jnp.int32, (1, lanes), 1) & (RB - 1))
        off = jnp.zeros((1, lanes), jnp.int32)
        first = jnp.zeros((1, lanes), jnp.int32) + rows
        max_off = jnp.int32(0)
        min_off = jnp.int32(plen)
        for i in range(4):
            lo, hi, n = slots[0, i], slots[1, i], slots[2, i]
            inside = (row >= lo) & (row < hi)
            off = jnp.where(inside, n, off)
            first = jnp.where(inside, lo, first)
            meets = (lo < r0 + RB) & (hi > r0)
            max_off = jnp.maximum(max_off, jnp.where(meets, n, 0))
            min_off = jnp.minimum(min_off, jnp.where(meets, n, plen))
        valid = off > 0
        n_all = (max_off + KC - 1) // KC
        n_free = jnp.minimum(min_off // KC, n_all)
        off = jnp.where(valid, off, plen)

        @pl.when(max_off == 0)
        def _():
            dq[pl.ds(r0, RB), :] = jnp.zeros((RB, width), dq.dtype)

        @pl.when(max_off > 0)
        def _():
            qb = jnp.concatenate([q[pl.ds(r0, RB), h * D:(h + 1) * D] for h in range(heads)], axis=0)
            db = jnp.concatenate([do[pl.ds(r0, RB), h * D:(h + 1) * D] for h in range(heads)], axis=0)
            qt, dt = qb.T, db.T
            w0 = pl.multiple_of(jnp.maximum(r0 - RB, 0), RB)

            def raw(kk, mask):
                t = lax.dot_general(kk, qb, NT, preferred_element_type=F32) * scale
                return t if mask is None else jnp.where(mask, t, NEG)

            def weigh(vv, at, slot, n, old, m, l, d):
                e = jnp.exp(groups(t_ref[pl.ds(0, n), :]) - m[None])
                mx_ref[slot] = m
                e_ref[pl.ds(at, n), :] = e.reshape(n, lanes).astype(jnp.bfloat16)
                dp = lax.dot_general(vv, db, NT, preferred_element_type=F32)
                dp_ref[pl.ds(at, n), :] = dp
                fade = jnp.exp(old - m)
                return l * fade + jnp.sum(e, axis=0), d * fade + jnp.sum(e * groups(dp), axis=0)

            def mask_at(at):
                return at + lax.broadcasted_iota(jnp.int32, (KC, lanes), 0) < off

            def piece(ref, c):
                return ref[pl.ds(pl.multiple_of(c * KC, KC), KC), :]

            def step_to(c, mask, carry):
                old, m, l, d = carry
                t = raw(piece(k, c), mask)
                l, d = weigh(piece(v, c - 1), pl.multiple_of((c - 1) * KC, KC), c - 1, KC, old, m, l, d)
                t_ref[...] = t
                return m, jnp.maximum(m, jnp.max(groups(t), axis=0)), l, d

            zero = jnp.zeros((8, lanes), F32)
            low = jnp.full((8, lanes), NEG, F32)
            near = pl.ds(w0, 2 * RB)
            last = plen // KC
            key = w0 + lax.broadcasted_iota(jnp.int32, (2 * RB, lanes), 0)
            first_t = raw(ck[near, :], (key >= first) & (key <= row))
            m = jnp.max(groups(first_t), axis=0)
            t_ref[pl.ds(0, 2 * RB), :] = first_t
            t = raw(piece(k, 0), None)
            l, d = weigh(cv[near, :], plen, last, 2 * RB, low, m, zero, zero)
            t_ref[...] = t
            carry = (m, jnp.maximum(m, jnp.max(groups(t), axis=0)), l, d)
            turn = jnp.maximum(n_free, 1)
            carry = lax.fori_loop(1, turn, lambda c, x: step_to(c, None, x), carry)
            carry = lax.fori_loop(turn, n_all, lambda c, x: step_to(c, mask_at(c * KC), x), carry)
            old, m, l, d = carry
            l, d = weigh(piece(v, n_all - 1), pl.multiple_of((n_all - 1) * KC, KC), n_all - 1, KC, old, m, l, d)

            top = jnp.max(m, axis=0, keepdims=True)
            fade = jnp.exp(m - top)
            inv = jnp.where(valid, 1.0 / jnp.sum(l * fade, axis=0, keepdims=True), 0.0)
            delta = jnp.sum(d * fade, axis=0, keepdims=True) * inv
            delta = jnp.broadcast_to(delta, (8, lanes))

            def grads(at, n, slot):
                g = (jnp.exp(mx_ref[slot] - top) * inv).astype(jnp.bfloat16)
                g = jnp.concatenate([g, g], axis=0)
                p = (e_ref[pl.ds(at, n), :].reshape(n // 16, 16, lanes) * g[None]).reshape(n, lanes)
                u = groups(dp_ref[pl.ds(at, n), :]) - delta[None]
                return p, p * u.reshape(n, lanes).astype(jnp.bfloat16)

            def products(c):
                at = pl.multiple_of(c * KC, KC)
                p, ds = p_ref[...], ds_ref[...]
                dvt[:, pl.ds(at, KC)] += lax.dot_general(dt, p, NT, preferred_element_type=F32)
                dkt[:, pl.ds(at, KC)] += lax.dot_general(qt, ds, NT, preferred_element_type=F32)
                gq_ref[...] += jnp.dot(kt_ref[:, pl.ds(at, KC)], ds, preferred_element_type=F32)

            def back(c, carry):
                products(c - 1)
                p_ref[...], ds_ref[...] = grads(pl.multiple_of(c * KC, KC), KC, c)
                return carry

            p, ds = grads(plen, 2 * RB, last)
            p_ref[...], ds_ref[...] = grads(0, KC, 0)
            dcva[near, :] += jnp.dot(p, db, preferred_element_type=F32)
            dcka[near, :] += jnp.dot(ds, qb, preferred_element_type=F32)
            gq_ref[...] = lax.dot_general(ck[near, :], ds, TN, preferred_element_type=F32)
            lax.fori_loop(1, n_all, back, 0)
            products(n_all - 1)
            gq = (gq_ref[...] * scale).T.astype(dq.dtype)
            for h in range(heads):
                dq[pl.ds(r0, RB), h * D:(h + 1) * D] = gq[h * RB:(h + 1) * RB, :]

        dq_copy(b).start()

    dck[...] = (dcka[...] * scale).astype(dck.dtype)
    dcv[...] = dcva[...].astype(dcv.dtype)
    stores = [pltpu.make_async_copy(dck, dck_out, out_sem.at[0]), pltpu.make_async_copy(dcv, dcv_out, out_sem.at[1])]
    for cp in stores:
        cp.start()
    for c in range(plen // KC):
        at = pl.ds(c * KC, KC)
        dk[at, :] = (dkt[:, at] * scale).T.astype(dk.dtype)
        dv[at, :] = dvt[:, at].T.astype(dv.dtype)
        for n, (src, dst) in enumerate(((dk, dk_out), (dv, dv_out))):
            cp = pltpu.make_async_copy(src.at[at, :], dst.at[at, :], out_sem.at[2 + 2 * c + n])
            cp.start()
            stores.append(cp)
    for b in range(rows // RB):
        dq_copy(b).wait()
    for cp in stores:
        cp.wait()


def attn_call(assign, lengths, offsets, q, do, ck, cv, kv):
    rows, width = q.shape
    plen = kv.shape[1]
    lanes = width // D * RB
    bf = jnp.bfloat16
    smem = pl.BlockSpec(memory_space=pltpu.SMEM)
    hbm = pl.BlockSpec(memory_space=pltpu.HBM)
    wide, thin, prompt = (rows, width), (rows, D), (plen, D)
    outs = (wide, thin, thin, prompt, prompt)
    return pl.pallas_call(
        attn_kernel,
        out_shape=tuple(jax.ShapeDtypeStruct(x, bf) for x in outs),
        in_specs=[smem] * 3 + [hbm] * 5,
        out_specs=[hbm] * 5,
        scratch_shapes=[pltpu.VMEM(x, bf) for x in (wide, wide, thin, thin, prompt, prompt) + outs] + [
            pltpu.SMEM((3, 8), jnp.int32),
            pltpu.VMEM((plen + 2 * RB, lanes), bf),
            pltpu.VMEM((plen + 2 * RB, lanes), F32),
            pltpu.VMEM((plen // KC + 1, 8, lanes), F32),
            pltpu.VMEM((D, plen), F32),
            pltpu.VMEM((D, plen), F32),
            pltpu.VMEM((rows, D), F32),
            pltpu.VMEM((rows, D), F32),
            pltpu.VMEM((KC, lanes), F32),
            pltpu.VMEM((KC, lanes), bf),
            pltpu.VMEM((KC, lanes), bf),
            pltpu.VMEM((D, lanes), F32),
            pltpu.VMEM((D, plen), bf),
            pltpu.SemaphoreType.DMA((6,)),
            pltpu.SemaphoreType.DMA((rows // RB,)),
            pltpu.SemaphoreType.DMA((2 + 2 * (plen // KC),)),
        ],
        compiler_params=pltpu.CompilerParams(vmem_limit_bytes=63 << 20),
    )(assign, lengths, offsets, q, do, ck, cv, kv)


def per_device(query, grad_out, continuation_key, continuation_value, prompt_key, shared_prompt_value, assign, lengths, offsets):
    prompt = gather(prompt_key, shared_prompt_value)
    query_grad, key_grad, value_grad, dk, dv = attn_call(
        assign, lengths, offsets, query, grad_out, continuation_key, continuation_value, prompt
    )
    prompt_key_grad, prompt_value_grad = reduce(dk, dv)
    return query_grad, key_grad, value_grad, prompt_key_grad, prompt_value_grad


def solution(mesh):
    rows = P("cand", "prefix")
    owned = P(("prefix", "cand"), None)
    return jax.shard_map(
        per_device,
        mesh=mesh,
        in_specs=(rows, rows, rows, rows, owned, owned, P(), P(), P()),
        out_specs=(rows, rows, rows, owned, owned),
        check_vma=False,
    )
```

```python
import functools
import math

import jax
import jax.numpy as jnp
from jax import lax
from jax.experimental import pallas as pl
from jax.experimental.pallas import tpu as pltpu
from jax.sharding import PartitionSpec as P

D = 128
MESH = pl.DeviceIdType.MESH
ALL = pl.ds(0, 8)
HEADS_FAR = [(2, 1), (2, 0), (1, 1), (3, 1), (1, 0), (3, 0), (0, 1), (0, 0)]
GROUPS = [
    [(2, dz, dy, dl) for dz in (1, 0) for dy, dl in HEADS_FAR],
    [(1, dz, dy, dl) for dz in (1, 0) for dy, dl in HEADS_FAR],
    [(3, dz, dy, dl) for dz in (1, 0) for dy, dl in HEADS_FAR],
    [(0, 1, dy, dl) for dy, dl in HEADS_FAR],
    [(0, 0, dy, dl) for dy, dl in HEADS_FAR[:-1]],
]


class Place:
    def __init__(self):
        self.p, self.c = lax.axis_index("prefix"), lax.axis_index("cand")
        self.x, self.zh, self.co = self.c // 4, (self.c // 2) % 2, self.c % 2
        self.zl, self.y = self.p // 4, self.p % 4
        self.partner = (self.p, self.c + 1 - 2 * self.co)

    def head(self, dy, dl):
        return ((self.zl + dl) % 2) * 4 + (self.y + dy) % 4

    def chip(self, dx, dz):
        return (self.x + dx) % 4, (self.zh + dz) % 2

    def peer(self, dx, dz, dy, dl):
        x, zh = self.chip(dx, dz)
        return (self.head(dy, dl), x * 4 + zh * 2 + self.co)


def greet(at):
    barrier = pltpu.get_barrier_semaphore()
    n = 1
    pl.semaphore_signal(barrier, inc=1, device_id=at.partner, device_id_type=MESH)
    for group in GROUPS:
        for offset in group:
            n += 1
            pl.semaphore_signal(barrier, inc=1, device_id=at.peer(*offset), device_id_type=MESH)
    pl.semaphore_wait(barrier, n)


def remote(src, dst, send, recv, peer):
    return pltpu.make_async_remote_copy(src_ref=src, dst_ref=dst, send_sem=send, recv_sem=recv, device_id=peer, device_id_type=MESH)


def columns(head):
    return pl.ds(pl.multiple_of(head * D, D), D)


def gather_kernel(pk, pv, full, stage, send, recv, send_near, recv_near, send_core, recv_core, own_sem):
    at = Place()
    staged = []
    for a, src in enumerate((pk, pv)):
        cp = pltpu.make_async_copy(src, stage.at[a], own_sem.at[a])
        cp.start()
        staged.append(cp)
    greet(at)
    for cp in staged:
        cp.wait()
    near = []
    for g, group in enumerate(GROUPS):
        for i, offset in enumerate(group):
            peer = at.peer(*offset)
            s, r = (send.at[g], recv.at[g]) if g < 4 else (send_near.at[i], recv_near.at[i])
            cp = remote(stage.at[:, :, columns(peer[0])], full.at[:, at.p, at.x, at.zh, at.co], s, r, peer)
            cp.start()
            if g == 4:
                near.append(cp)
    own = pltpu.make_async_copy(stage.at[:, :, columns(at.p)], full.at[:, at.p, at.x, at.zh, at.co], own_sem.at[2])
    own.start()
    regions = [(at.chip(2, 0)[0], pl.ds(0, 2)), (at.chip(3, 0)[0], pl.ds(0, 2)), (at.chip(1, 0)[0], pl.ds(0, 2)), (at.x, 1 - at.zh), (at.x, at.zh)]
    handed = []

    def hand(g):
        ref = full.at[:, ALL, regions[g][0], regions[g][1], at.co]
        cp = remote(ref, ref, send_core.at[g], recv_core.at[g], at.partner)
        cp.start()
        handed.append(cp)

    bulk = []
    for g in range(4):
        ref = full.at[:, ALL, regions[g][0], regions[g][1], at.co]
        cp = remote(ref, ref, send.at[g], recv.at[g], at.partner)
        cp.wait_recv()
        bulk.append(cp)
        hand(g)
    for cp in near:
        cp.wait_recv()
    own.wait()
    hand(4)
    for cp in handed:
        cp.wait_recv()
    for cp in bulk + near + handed:
        cp.wait_send()


def gather(pk, pv):
    rows = pk.shape[0]
    hbm = pl.BlockSpec(memory_space=pltpu.HBM)
    dma = lambda *s: pltpu.SemaphoreType.DMA(s)
    full = pl.pallas_call(
        gather_kernel,
        out_shape=jax.ShapeDtypeStruct((2, 8, 4, 2, 2, rows, D), pk.dtype),
        in_specs=[hbm] * 2,
        out_specs=hbm,
        scratch_shapes=[pltpu.VMEM((2, rows, 8 * D), pk.dtype), dma(4), dma(4), dma(7), dma(7), dma(5), dma(5), dma(3)],
        compiler_params=pltpu.CompilerParams(collective_id=0, has_side_effects=True),
    )(pk, pv)
    return full.reshape(2, -1, D)


def reduce_kernel(dk, dv, ok, ov, mine, other, part, came, send, recv, send_near, recv_near, send_core, recv_core, own_sem):
    at = Place()
    f32 = jnp.float32
    order = [at.chip(2, 0)[0], at.chip(1, 0)[0], at.chip(3, 0)[0], at.x]
    loads = []
    for i, x in enumerate(order):
        for a, src in enumerate((dk, dv)):
            cp = pltpu.make_async_copy(src.at[:, x, :, at.co], mine.at[a, i], own_sem.at[a, i])
            cp.start()
            loads.append(cp)
    greet(at)
    crossed = []
    for i, x in enumerate(order):
        for a, src in enumerate((dk, dv)):
            cp = remote(src.at[:, x, :, 1 - at.co], other.at[a, i], send_core.at[a, i], recv_core.at[a, i], at.partner)
            cp.start()
            crossed.append(cp)
    near = []
    slot = at.x * 2 + at.zh
    for i in range(4):
        for a in range(2):
            loads[2 * i + a].wait()
            crossed[2 * i + a].wait_recv()
            part[a, i] = (mine[a, i].astype(f32) + other[a, i].astype(f32)).astype(part.dtype)
            for g in ((i,) if i < 3 else (3, 4)):
                for j, offset in enumerate(GROUPS[g]):
                    peer = at.peer(*offset)
                    s, r = (send.at[a, g], recv.at[a, g]) if g < 4 else (send_near.at[a, j], recv_near.at[a, j])
                    zh = at.chip(0, offset[1])[1]
                    cp = remote(part.at[a, i, peer[0], zh], came.at[a, slot, :, columns(at.p)], s, r, peer)
                    cp.start()
                    if g == 4:
                        near.append(cp)
    own = []
    for a in range(2):
        cp = pltpu.make_async_copy(part.at[a, 3, at.p, at.zh], came.at[a, slot, :, columns(at.p)], own_sem.at[a, 4])
        cp.start()
        own.append(cp)
    bulk = []
    for g in range(4):
        for a in range(2):
            ref = mine.at[a, g] if g < 3 else mine.at[a, g, :, 0]
            cp = remote(ref, ref, send.at[a, g], recv.at[a, g], at.partner)
            cp.wait_recv()
            bulk.append(cp)
    for cp in near:
        cp.wait_recv()
    for cp in own:
        cp.wait()
    for a, out in enumerate((ok, ov)):
        total = came[a, 0].astype(f32)
        for s in range(1, 8):
            total += came[a, s].astype(f32)
        out[...] = total.astype(out.dtype)
    for cp in crossed + bulk + near:
        cp.wait_send()


def reduce(dk, dv):
    rows = dk.shape[0] // 128
    bf = dk.dtype
    shape = (8, 4, 2, 2, rows, D)
    out = jax.ShapeDtypeStruct((rows, 8 * D), bf)
    dma = lambda *s: pltpu.SemaphoreType.DMA(s)
    buf = pltpu.VMEM((2, 4, 8, 2, rows, D), bf)
    return pl.pallas_call(
        reduce_kernel,
        out_shape=(out, out),
        in_specs=[pl.BlockSpec(memory_space=pltpu.HBM)] * 2,
        out_specs=[pl.BlockSpec(memory_space=pltpu.VMEM)] * 2,
        scratch_shapes=[buf, buf, buf, pltpu.VMEM((2, 8, rows, 8 * D), bf),
                        dma(2, 4), dma(2, 4), dma(2, 7), dma(2, 7), dma(2, 4), dma(2, 4), dma(2, 5)],
        compiler_params=pltpu.CompilerParams(collective_id=1, has_side_effects=True, vmem_limit_bytes=56_000_000),
    )(dk.reshape(shape), dv.reshape(shape))


KC = 512
HC = 256
RB = 64
NEG = -1e30
NT = (((1,), (1,)), ((), ()))
TN = (((0,), (0,)), ((), ()))
F32 = jnp.float32


def groups(x):
    return x.reshape(x.shape[0] // 8, 8, x.shape[1])


def attn_kernel(assign, lengths, offsets, q_in, do_in, ck_in, cv_in, kv, dq_out, dck_out, dcv_out, dk_out, dv_out,
                q, do, ck, cv, k, v, dq, dck, dcv, dk, dv, slots, e_ref, dp_ref, mx_ref, dkt, dvt, dcka, dcva,
                t_ref, p_ref, ds_ref, gq_ref, kt_ref, in_sem, dq_sem, out_sem):
    rows, width = q.shape
    heads = width // D
    plen = k.shape[0]
    lanes = heads * RB
    scale = 1.0 / math.sqrt(D)
    cand = lax.axis_index("cand")

    loads = [
        pltpu.make_async_copy(src, dst, in_sem.at[n])
        for n, (src, dst) in enumerate(((kv.at[0], k), (kv.at[1], v), (q_in, q), (do_in, do), (ck_in, ck), (cv_in, cv)))
    ]
    for cp in loads:
        cp.start()

    def place_rows(i, carry):
        slot, start = carry
        slots[0, slot] = start
        slots[1, slot] = start + lengths[i]
        slots[2, slot] = offsets[i]
        hit = assign[i] == cand
        return (jnp.where(hit, slot + 1, slot), jnp.where(hit, start + lengths[i], start))

    lax.fori_loop(0, assign.shape[0], place_rows, (jnp.int32(0), jnp.int32(0)), unroll=8)
    dkt[...] = jnp.zeros_like(dkt)
    dvt[...] = jnp.zeros_like(dvt)
    dcka[...] = jnp.zeros_like(dcka)
    dcva[...] = jnp.zeros_like(dcva)
    loads[0].wait()

    @pl.loop(0, plen // KC)
    def _(c):
        at = pl.multiple_of(c * KC, KC)
        kt_ref[:, pl.ds(at, KC)] = k[pl.ds(at, KC), :].T

    for cp in loads[1:]:
        cp.wait()

    def dq_copy(b):
        band = pl.ds(pl.multiple_of(b * RB, RB), RB)
        return pltpu.make_async_copy(dq.at[band, :], dq_out.at[band, :], dq_sem.at[b])

    @pl.loop(0, rows // RB)
    def _(b):
        r0 = pl.multiple_of(b * RB, RB)
        row = r0 + (lax.broadcasted_iota(jnp.int32, (1, lanes), 1) & (RB - 1))
        off = jnp.zeros((1, lanes), jnp.int32)
        first = jnp.zeros((1, lanes), jnp.int32) + rows
        max_off = jnp.int32(0)
        min_off = jnp.int32(plen)
        for i in range(4):
            lo, hi, n = slots[0, i], slots[1, i], slots[2, i]
            inside = (row >= lo) & (row < hi)
            off = jnp.where(inside, n, off)
            first = jnp.where(inside, lo, first)
            meets = (lo < r0 + RB) & (hi > r0)
            max_off = jnp.maximum(max_off, jnp.where(meets, n, 0))
            min_off = jnp.minimum(min_off, jnp.where(meets, n, plen))
        valid = off > 0
        n_all = (max_off + KC - HC - 1) // KC
        half = max_off > n_all * KC
        n_free = jnp.minimum(min_off // KC, n_all)
        off = jnp.where(valid, off, plen)

        @pl.when(max_off == 0)
        def _():
            dq[pl.ds(r0, RB), :] = jnp.zeros((RB, width), dq.dtype)

        @pl.when(max_off > 0)
        def _():
            qb = jnp.concatenate([q[pl.ds(r0, RB), h * D:(h + 1) * D] for h in range(heads)], axis=0)
            db = jnp.concatenate([do[pl.ds(r0, RB), h * D:(h + 1) * D] for h in range(heads)], axis=0)
            qt, dt = qb.T, db.T
            w0 = pl.multiple_of(jnp.maximum(r0 - RB, 0), RB)

            def raw(kk, mask):
                t = lax.dot_general(kk, qb, NT, preferred_element_type=F32) * scale
                return t if mask is None else jnp.where(mask, t, NEG)

            def weigh(vv, at, slot, n, old, m, l, d):
                e = jnp.exp(groups(t_ref[pl.ds(0, n), :]) - m[None])
                mx_ref[slot] = m
                e_ref[pl.ds(at, n), :] = e.reshape(n, lanes).astype(jnp.bfloat16)
                dp = lax.dot_general(vv, db, NT, preferred_element_type=F32)
                dp_ref[pl.ds(at, n), :] = dp
                fade = jnp.exp(old - m)
                return l * fade + jnp.sum(e, axis=0), d * fade + jnp.sum(e * groups(dp), axis=0)

            def mask_at(at):
                return at + lax.broadcasted_iota(jnp.int32, (KC, lanes), 0) < off

            def piece(ref, c):
                return ref[pl.ds(pl.multiple_of(c * KC, KC), KC), :]

            def step_to(c, mask, carry):
                old, m, l, d = carry
                t = raw(piece(k, c), mask)
                l, d = weigh(piece(v, c - 1), pl.multiple_of((c - 1) * KC, KC), c - 1, KC, old, m, l, d)
                t_ref[...] = t
                return m, jnp.maximum(m, jnp.max(groups(t), axis=0)), l, d

            zero = jnp.zeros((8, lanes), F32)
            low = jnp.full((8, lanes), NEG, F32)
            near = pl.ds(w0, 2 * RB)
            last = plen // KC
            key = w0 + lax.broadcasted_iota(jnp.int32, (2 * RB, lanes), 0)
            first_t = raw(ck[near, :], (key >= first) & (key <= row))
            m = jnp.max(groups(first_t), axis=0)
            t_ref[pl.ds(0, 2 * RB), :] = first_t
            t = raw(piece(k, 0), None)
            l, d = weigh(cv[near, :], plen, last, 2 * RB, low, m, zero, zero)
            t_ref[...] = t
            carry = (m, jnp.maximum(m, jnp.max(groups(t), axis=0)), l, d)
            turn = jnp.maximum(n_free, 1)
            carry = lax.fori_loop(1, turn, lambda c, x: step_to(c, None, x), carry)
            carry = lax.fori_loop(turn, n_all, lambda c, x: step_to(c, mask_at(c * KC), x), carry)
            old, m, l, d = carry
            tail = pl.multiple_of(n_all * KC, KC)

            def end_half(_):
                t = raw(k[pl.ds(tail, HC), :], tail + lax.broadcasted_iota(jnp.int32, (HC, lanes), 0) < off)
                l1, d1 = weigh(piece(v, n_all - 1), pl.multiple_of((n_all - 1) * KC, KC), n_all - 1, KC, old, m, l, d)
                t_ref[pl.ds(0, HC), :] = t
                m1 = jnp.maximum(m, jnp.max(groups(t), axis=0))
                l1, d1 = weigh(v[pl.ds(tail, HC), :], tail, n_all, HC, m, m1, l1, d1)
                return m1, l1, d1

            def end_whole(_):
                l1, d1 = weigh(piece(v, n_all - 1), pl.multiple_of((n_all - 1) * KC, KC), n_all - 1, KC, old, m, l, d)
                return m, l1, d1

            m, l, d = lax.cond(half, end_half, end_whole, 0)

            top = jnp.max(m, axis=0, keepdims=True)
            fade = jnp.exp(m - top)
            inv = jnp.where(valid, 1.0 / jnp.sum(l * fade, axis=0, keepdims=True), 0.0)
            delta = jnp.sum(d * fade, axis=0, keepdims=True) * inv
            delta = jnp.broadcast_to(delta, (8, lanes))

            def grads(at, n, slot):
                g = (jnp.exp(mx_ref[slot] - top) * inv).astype(jnp.bfloat16)
                g = jnp.concatenate([g, g], axis=0)
                p = (e_ref[pl.ds(at, n), :].reshape(n // 16, 16, lanes) * g[None]).reshape(n, lanes)
                u = groups(dp_ref[pl.ds(at, n), :]) - delta[None]
                return p, p * u.reshape(n, lanes).astype(jnp.bfloat16)

            def products(c):
                at = pl.multiple_of(c * KC, KC)
                p, ds = p_ref[...], ds_ref[...]
                dvt[:, pl.ds(at, KC)] += lax.dot_general(dt, p, NT, preferred_element_type=F32)
                dkt[:, pl.ds(at, KC)] += lax.dot_general(qt, ds, NT, preferred_element_type=F32)
                gq_ref[...] += jnp.dot(kt_ref[:, pl.ds(at, KC)], ds, preferred_element_type=F32)

            def back(c, carry):
                products(c - 1)
                p_ref[...], ds_ref[...] = grads(pl.multiple_of(c * KC, KC), KC, c)
                return carry

            p, ds = grads(plen, 2 * RB, last)
            p_ref[...], ds_ref[...] = grads(0, KC, 0)
            dcva[near, :] += jnp.dot(p, db, preferred_element_type=F32)
            dcka[near, :] += jnp.dot(ds, qb, preferred_element_type=F32)
            gq_ref[...] = lax.dot_general(ck[near, :], ds, TN, preferred_element_type=F32)
            lax.fori_loop(1, n_all, back, 0)
            products(n_all - 1)

            @pl.when(half)
            def _():
                at = pl.ds(tail, HC)
                p, ds = grads(tail, HC, n_all)
                dvt[:, at] += lax.dot_general(dt, p, NT, preferred_element_type=F32)
                dkt[:, at] += lax.dot_general(qt, ds, NT, preferred_element_type=F32)
                gq_ref[...] += jnp.dot(kt_ref[:, at], ds, preferred_element_type=F32)

            gq = (gq_ref[...] * scale).T.astype(dq.dtype)
            for h in range(heads):
                dq[pl.ds(r0, RB), h * D:(h + 1) * D] = gq[h * RB:(h + 1) * RB, :]

        dq_copy(b).start()

    dck[...] = (dcka[...] * scale).astype(dck.dtype)
    dcv[...] = dcva[...].astype(dcv.dtype)
    stores = [pltpu.make_async_copy(dck, dck_out, out_sem.at[0]), pltpu.make_async_copy(dcv, dcv_out, out_sem.at[1])]
    for cp in stores:
        cp.start()
    for c in range(plen // KC):
        at = pl.ds(c * KC, KC)
        dk[at, :] = (dkt[:, at] * scale).T.astype(dk.dtype)
        dv[at, :] = dvt[:, at].T.astype(dv.dtype)
        for n, (src, dst) in enumerate(((dk, dk_out), (dv, dv_out))):
            cp = pltpu.make_async_copy(src.at[at, :], dst.at[at, :], out_sem.at[2 + 2 * c + n])
            cp.start()
            stores.append(cp)
    for b in range(rows // RB):
        dq_copy(b).wait()
    for cp in stores:
        cp.wait()


def attn_call(assign, lengths, offsets, q, do, ck, cv, kv):
    rows, width = q.shape
    plen = kv.shape[1]
    lanes = width // D * RB
    bf = jnp.bfloat16
    smem = pl.BlockSpec(memory_space=pltpu.SMEM)
    hbm = pl.BlockSpec(memory_space=pltpu.HBM)
    wide, thin, prompt = (rows, width), (rows, D), (plen, D)
    outs = (wide, thin, thin, prompt, prompt)
    return pl.pallas_call(
        attn_kernel,
        out_shape=tuple(jax.ShapeDtypeStruct(x, bf) for x in outs),
        in_specs=[smem] * 3 + [hbm] * 5,
        out_specs=[hbm] * 5,
        scratch_shapes=[pltpu.VMEM(x, bf) for x in (wide, wide, thin, thin, prompt, prompt) + outs] + [
            pltpu.SMEM((3, 8), jnp.int32),
            pltpu.VMEM((plen + 2 * RB, lanes), bf),
            pltpu.VMEM((plen + 2 * RB, lanes), F32),
            pltpu.VMEM((plen // KC + 1, 8, lanes), F32),
            pltpu.VMEM((D, plen), F32),
            pltpu.VMEM((D, plen), F32),
            pltpu.VMEM((rows, D), F32),
            pltpu.VMEM((rows, D), F32),
            pltpu.VMEM((KC, lanes), F32),
            pltpu.VMEM((KC, lanes), bf),
            pltpu.VMEM((KC, lanes), bf),
            pltpu.VMEM((D, lanes), F32),
            pltpu.VMEM((D, plen), bf),
            pltpu.SemaphoreType.DMA((6,)),
            pltpu.SemaphoreType.DMA((rows // RB,)),
            pltpu.SemaphoreType.DMA((2 + 2 * (plen // KC),)),
        ],
        compiler_params=pltpu.CompilerParams(vmem_limit_bytes=63 << 20),
    )(assign, lengths, offsets, q, do, ck, cv, kv)


def per_device(query, grad_out, continuation_key, continuation_value, prompt_key, shared_prompt_value, assign, lengths, offsets):
    prompt = gather(prompt_key, shared_prompt_value)
    query_grad, key_grad, value_grad, dk, dv = attn_call(
        assign, lengths, offsets, query, grad_out, continuation_key, continuation_value, prompt
    )
    prompt_key_grad, prompt_value_grad = reduce(dk, dv)
    return query_grad, key_grad, value_grad, prompt_key_grad, prompt_value_grad


def solution(mesh):
    rows = P("cand", "prefix")
    owned = P(("prefix", "cand"), None)
    return jax.shard_map(
        per_device,
        mesh=mesh,
        in_specs=(rows, rows, rows, rows, owned, owned, P(), P(), P()),
        out_specs=(rows, rows, rows, owned, owned),
        check_vma=False,
    )
```

```python
import functools
import math

import jax
import jax.numpy as jnp
from jax import lax
from jax.experimental import pallas as pl
from jax.experimental.pallas import tpu as pltpu
from jax.sharding import PartitionSpec as P

D = 128
MESH = pl.DeviceIdType.MESH
ALL = pl.ds(0, 8)
HEADS_FAR = [(2, 1), (2, 0), (1, 1), (3, 1), (1, 0), (3, 0), (0, 1), (0, 0)]
GROUPS = [
    [(2, dz, dy, dl) for dz in (1, 0) for dy, dl in HEADS_FAR],
    [(1, dz, dy, dl) for dz in (1, 0) for dy, dl in HEADS_FAR],
    [(3, dz, dy, dl) for dz in (1, 0) for dy, dl in HEADS_FAR],
    [(0, 1, dy, dl) for dy, dl in HEADS_FAR],
    [(0, 0, dy, dl) for dy, dl in HEADS_FAR[:-1]],
]


class Place:
    def __init__(self):
        self.p, self.c = lax.axis_index("prefix"), lax.axis_index("cand")
        self.x, self.zh, self.co = self.c // 4, (self.c // 2) % 2, self.c % 2
        self.zl, self.y = self.p // 4, self.p % 4
        self.partner = (self.p, self.c + 1 - 2 * self.co)

    def head(self, dy, dl):
        return ((self.zl + dl) % 2) * 4 + (self.y + dy) % 4

    def chip(self, dx, dz):
        return (self.x + dx) % 4, (self.zh + dz) % 2

    def peer(self, dx, dz, dy, dl):
        x, zh = self.chip(dx, dz)
        return (self.head(dy, dl), x * 4 + zh * 2 + self.co)


def greet(at):
    barrier = pltpu.get_barrier_semaphore()
    n = 1
    pl.semaphore_signal(barrier, inc=1, device_id=at.partner, device_id_type=MESH)
    for group in GROUPS:
        for offset in group:
            n += 1
            pl.semaphore_signal(barrier, inc=1, device_id=at.peer(*offset), device_id_type=MESH)
    pl.semaphore_wait(barrier, n)


def remote(src, dst, send, recv, peer):
    return pltpu.make_async_remote_copy(src_ref=src, dst_ref=dst, send_sem=send, recv_sem=recv, device_id=peer, device_id_type=MESH)


def columns(head):
    return pl.ds(pl.multiple_of(head * D, D), D)


def gather_kernel(pk, pv, full, stage, send, recv, send_near, recv_near, send_core, recv_core, own_sem):
    at = Place()
    staged = []
    for a, src in enumerate((pk, pv)):
        cp = pltpu.make_async_copy(src, stage.at[a], own_sem.at[a])
        cp.start()
        staged.append(cp)
    greet(at)
    for cp in staged:
        cp.wait()
    near = []
    for g, group in enumerate(GROUPS):
        for i, offset in enumerate(group):
            peer = at.peer(*offset)
            s, r = (send.at[g], recv.at[g]) if g < 4 else (send_near.at[i], recv_near.at[i])
            cp = remote(stage.at[:, :, columns(peer[0])], full.at[:, at.p, at.x, at.zh, at.co], s, r, peer)
            cp.start()
            if g == 4:
                near.append(cp)
    own = pltpu.make_async_copy(stage.at[:, :, columns(at.p)], full.at[:, at.p, at.x, at.zh, at.co], own_sem.at[2])
    own.start()
    regions = [(at.chip(2, 0)[0], pl.ds(0, 2)), (at.chip(3, 0)[0], pl.ds(0, 2)), (at.chip(1, 0)[0], pl.ds(0, 2)), (at.x, 1 - at.zh), (at.x, at.zh)]
    handed = []

    def hand(g):
        ref = full.at[:, ALL, regions[g][0], regions[g][1], at.co]
        cp = remote(ref, ref, send_core.at[g], recv_core.at[g], at.partner)
        cp.start()
        handed.append(cp)

    bulk = []
    for g in range(4):
        ref = full.at[:, ALL, regions[g][0], regions[g][1], at.co]
        cp = remote(ref, ref, send.at[g], recv.at[g], at.partner)
        cp.wait_recv()
        bulk.append(cp)
        hand(g)
    for cp in near:
        cp.wait_recv()
    own.wait()
    hand(4)
    for cp in handed:
        cp.wait_recv()
    for cp in bulk + near + handed:
        cp.wait_send()


def gather(pk, pv):
    rows = pk.shape[0]
    hbm = pl.BlockSpec(memory_space=pltpu.HBM)
    dma = lambda *s: pltpu.SemaphoreType.DMA(s)
    full = pl.pallas_call(
        gather_kernel,
        out_shape=jax.ShapeDtypeStruct((2, 8, 4, 2, 2, rows, D), pk.dtype),
        in_specs=[hbm] * 2,
        out_specs=hbm,
        scratch_shapes=[pltpu.VMEM((2, rows, 8 * D), pk.dtype), dma(4), dma(4), dma(7), dma(7), dma(5), dma(5), dma(3)],
        compiler_params=pltpu.CompilerParams(collective_id=0, has_side_effects=True),
    )(pk, pv)
    return full.reshape(2, -1, D)


def reduce_kernel(dk, dv, ok, ov, mine, other, part, came, send, recv, send_near, recv_near, send_core, recv_core, own_sem):
    at = Place()
    f32 = jnp.float32
    order = [at.chip(2, 0)[0], at.chip(1, 0)[0], at.chip(3, 0)[0], at.x]
    loads = []
    for i, x in enumerate(order):
        for a, src in enumerate((dk, dv)):
            cp = pltpu.make_async_copy(src.at[:, x, :, at.co], mine.at[a, i], own_sem.at[a, i])
            cp.start()
            loads.append(cp)
    greet(at)
    crossed = []
    for i, x in enumerate(order):
        for a, src in enumerate((dk, dv)):
            cp = remote(src.at[:, x, :, 1 - at.co], other.at[a, i], send_core.at[a, i], recv_core.at[a, i], at.partner)
            cp.start()
            crossed.append(cp)
    near = []
    slot = at.x * 2 + at.zh
    for i in range(4):
        for a in range(2):
            loads[2 * i + a].wait()
            crossed[2 * i + a].wait_recv()
            part[a, i] = (mine[a, i].astype(f32) + other[a, i].astype(f32)).astype(part.dtype)
            for g in ((i,) if i < 3 else (3, 4)):
                for j, offset in enumerate(GROUPS[g]):
                    peer = at.peer(*offset)
                    s, r = (send.at[a, g], recv.at[a, g]) if g < 4 else (send_near.at[a, j], recv_near.at[a, j])
                    zh = at.chip(0, offset[1])[1]
                    cp = remote(part.at[a, i, peer[0], zh], came.at[a, slot, :, columns(at.p)], s, r, peer)
                    cp.start()
                    if g == 4:
                        near.append(cp)
    own = []
    for a in range(2):
        cp = pltpu.make_async_copy(part.at[a, 3, at.p, at.zh], came.at[a, slot, :, columns(at.p)], own_sem.at[a, 4])
        cp.start()
        own.append(cp)
    bulk = []
    for g in range(4):
        for a in range(2):
            ref = mine.at[a, g] if g < 3 else mine.at[a, g, :, 0]
            cp = remote(ref, ref, send.at[a, g], recv.at[a, g], at.partner)
            cp.wait_recv()
            bulk.append(cp)
    for cp in near:
        cp.wait_recv()
    for cp in own:
        cp.wait()
    for a, out in enumerate((ok, ov)):
        total = came[a, 0].astype(f32)
        for s in range(1, 8):
            total += came[a, s].astype(f32)
        out[...] = total.astype(out.dtype)
    for cp in crossed + bulk + near:
        cp.wait_send()


def reduce(dk, dv):
    rows = dk.shape[0] // 128
    bf = dk.dtype
    shape = (8, 4, 2, 2, rows, D)
    out = jax.ShapeDtypeStruct((rows, 8 * D), bf)
    dma = lambda *s: pltpu.SemaphoreType.DMA(s)
    buf = pltpu.VMEM((2, 4, 8, 2, rows, D), bf)
    return pl.pallas_call(
        reduce_kernel,
        out_shape=(out, out),
        in_specs=[pl.BlockSpec(memory_space=pltpu.HBM)] * 2,
        out_specs=[pl.BlockSpec(memory_space=pltpu.VMEM)] * 2,
        scratch_shapes=[buf, buf, buf, pltpu.VMEM((2, 8, rows, 8 * D), bf),
                        dma(2, 4), dma(2, 4), dma(2, 7), dma(2, 7), dma(2, 4), dma(2, 4), dma(2, 5)],
        compiler_params=pltpu.CompilerParams(collective_id=1, has_side_effects=True, vmem_limit_bytes=56_000_000),
    )(dk.reshape(shape), dv.reshape(shape))


KC = 512
HC = 256
RB = 64
NEG = -1e30
NT = (((1,), (1,)), ((), ()))
TN = (((0,), (0,)), ((), ()))
F32 = jnp.float32


def groups(x):
    return x.reshape(x.shape[0] // 8, 8, x.shape[1])


def attn_kernel(assign, lengths, offsets, q_in, do_in, ck_in, cv_in, kv, dq_out, dck_out, dcv_out, dk_out, dv_out,
                q, do, ck, cv, k, v, dq, dck, dcv, dk, dv, slots, e_ref, dp_ref, mx_ref, dkt, dvt, dcka, dcva,
                t_ref, p_ref, ds_ref, gq_ref, kt_ref, in_sem, dq_sem, out_sem):
    rows, width = q.shape
    heads = width // D
    plen = k.shape[0]
    lanes = heads * RB
    scale = 1.0 / math.sqrt(D)
    cand = lax.axis_index("cand")

    loads = [
        pltpu.make_async_copy(src, dst, in_sem.at[n])
        for n, (src, dst) in enumerate(((kv.at[0], k), (kv.at[1], v), (q_in, q), (do_in, do), (ck_in, ck), (cv_in, cv)))
    ]
    for cp in loads:
        cp.start()

    def place_rows(i, carry):
        slot, start = carry
        slots[0, slot] = start
        slots[1, slot] = start + lengths[i]
        slots[2, slot] = offsets[i]
        hit = assign[i] == cand
        return (jnp.where(hit, slot + 1, slot), jnp.where(hit, start + lengths[i], start))

    lax.fori_loop(0, assign.shape[0], place_rows, (jnp.int32(0), jnp.int32(0)), unroll=8)
    dkt[...] = jnp.zeros_like(dkt)
    dvt[...] = jnp.zeros_like(dvt)
    dcka[...] = jnp.zeros_like(dcka)
    dcva[...] = jnp.zeros_like(dcva)
    loads[0].wait()

    @pl.loop(0, plen // KC)
    def _(c):
        at = pl.multiple_of(c * KC, KC)
        kt_ref[:, pl.ds(at, KC)] = k[pl.ds(at, KC), :].T

    for cp in loads[1:]:
        cp.wait()

    def dq_copy(b):
        band = pl.ds(pl.multiple_of(b * RB, RB), RB)
        return pltpu.make_async_copy(dq.at[band, :], dq_out.at[band, :], dq_sem.at[b])

    @pl.loop(0, rows // RB)
    def _(b):
        r0 = pl.multiple_of(b * RB, RB)
        row = r0 + (lax.broadcasted_iota(jnp.int32, (1, lanes), 1) & (RB - 1))
        off = jnp.zeros((1, lanes), jnp.int32)
        first = jnp.zeros((1, lanes), jnp.int32) + rows
        max_off = jnp.int32(0)
        min_off = jnp.int32(plen)
        for i in range(4):
            lo, hi, n = slots[0, i], slots[1, i], slots[2, i]
            inside = (row >= lo) & (row < hi)
            off = jnp.where(inside, n, off)
            first = jnp.where(inside, lo, first)
            meets = (lo < r0 + RB) & (hi > r0)
            max_off = jnp.maximum(max_off, jnp.where(meets, n, 0))
            min_off = jnp.minimum(min_off, jnp.where(meets, n, plen))
        valid = off > 0
        n_all = (max_off + KC - HC - 1) // KC
        half = max_off > n_all * KC
        n_free = jnp.minimum(min_off // KC, n_all)
        off = jnp.where(valid, off, plen)

        @pl.when(max_off == 0)
        def _():
            dq[pl.ds(r0, RB), :] = jnp.zeros((RB, width), dq.dtype)

        @pl.when(max_off > 0)
        def _():
            qb = jnp.concatenate([q[pl.ds(r0, RB), h * D:(h + 1) * D] for h in range(heads)], axis=0)
            db = jnp.concatenate([do[pl.ds(r0, RB), h * D:(h + 1) * D] for h in range(heads)], axis=0)
            w0 = pl.multiple_of(jnp.maximum(r0 - RB, 0), RB)

            def raw(kk, mask):
                t = lax.dot_general(kk, qb, NT, preferred_element_type=F32) * scale
                return t if mask is None else jnp.where(mask, t, NEG)

            def weigh(vv, at, slot, n, old, m, l, d):
                e = jnp.exp(groups(t_ref[pl.ds(0, n), :]) - m[None])
                mx_ref[slot] = m
                e_ref[pl.ds(at, n), :] = e.reshape(n, lanes).astype(jnp.bfloat16)
                dp = lax.dot_general(vv, db, NT, preferred_element_type=F32)
                dp_ref[pl.ds(at, n), :] = dp
                fade = jnp.exp(old - m)
                return l * fade + jnp.sum(e, axis=0), d * fade + jnp.sum(e * groups(dp), axis=0)

            def mask_at(at):
                return at + lax.broadcasted_iota(jnp.int32, (KC, lanes), 0) < off

            def piece(ref, c):
                return ref[pl.ds(pl.multiple_of(c * KC, KC), KC), :]

            def step_to(c, mask, carry):
                old, m, l, d = carry
                t = raw(piece(k, c), mask)
                l, d = weigh(piece(v, c - 1), pl.multiple_of((c - 1) * KC, KC), c - 1, KC, old, m, l, d)
                t_ref[...] = t
                return m, jnp.maximum(m, jnp.max(groups(t), axis=0)), l, d

            zero = jnp.zeros((8, lanes), F32)
            low = jnp.full((8, lanes), NEG, F32)
            near = pl.ds(w0, 2 * RB)
            last = plen // KC
            key = w0 + lax.broadcasted_iota(jnp.int32, (2 * RB, lanes), 0)
            first_t = raw(ck[near, :], (key >= first) & (key <= row))
            m = jnp.max(groups(first_t), axis=0)
            t_ref[pl.ds(0, 2 * RB), :] = first_t
            t = raw(piece(k, 0), None)
            l, d = weigh(cv[near, :], plen, last, 2 * RB, low, m, zero, zero)
            t_ref[...] = t
            carry = (m, jnp.maximum(m, jnp.max(groups(t), axis=0)), l, d)
            turn = jnp.maximum(n_free, 1)
            carry = lax.fori_loop(1, turn, lambda c, x: step_to(c, None, x), carry)
            carry = lax.fori_loop(turn, n_all, lambda c, x: step_to(c, mask_at(c * KC), x), carry)
            old, m, l, d = carry
            tail = pl.multiple_of(n_all * KC, KC)

            def end_half(_):
                t = raw(k[pl.ds(tail, HC), :], tail + lax.broadcasted_iota(jnp.int32, (HC, lanes), 0) < off)
                l1, d1 = weigh(piece(v, n_all - 1), pl.multiple_of((n_all - 1) * KC, KC), n_all - 1, KC, old, m, l, d)
                t_ref[pl.ds(0, HC), :] = t
                m1 = jnp.maximum(m, jnp.max(groups(t), axis=0))
                l1, d1 = weigh(v[pl.ds(tail, HC), :], tail, n_all, HC, m, m1, l1, d1)
                return m1, l1, d1

            def end_whole(_):
                l1, d1 = weigh(piece(v, n_all - 1), pl.multiple_of((n_all - 1) * KC, KC), n_all - 1, KC, old, m, l, d)
                return m, l1, d1

            m, l, d = lax.cond(half, end_half, end_whole, 0)

            top = jnp.max(m, axis=0, keepdims=True)
            fade = jnp.exp(m - top)
            inv = jnp.where(valid, 1.0 / jnp.sum(l * fade, axis=0, keepdims=True), 0.0)
            delta = jnp.sum(d * fade, axis=0, keepdims=True) * inv
            delta = jnp.broadcast_to(delta, (8, lanes))

            def grads(at, n, slot):
                g = (jnp.exp(mx_ref[slot] - top) * inv).astype(jnp.bfloat16)
                g = jnp.concatenate([g, g], axis=0)
                p = (e_ref[pl.ds(at, n), :].reshape(n // 16, 16, lanes) * g[None]).reshape(n, lanes)
                u = groups(dp_ref[pl.ds(at, n), :]) - delta[None]
                return p, p * u.reshape(n, lanes).astype(jnp.bfloat16)

            def products(c):
                at = pl.multiple_of(c * KC, KC)
                p, ds = p_ref[...], ds_ref[...]
                dvt[pl.ds(at, KC), :] += jnp.dot(p, db, preferred_element_type=F32)
                dkt[pl.ds(at, KC), :] += jnp.dot(ds, qb, preferred_element_type=F32)
                gq_ref[...] += jnp.dot(kt_ref[:, pl.ds(at, KC)], ds, preferred_element_type=F32)

            def back(c, carry):
                products(c - 1)
                p_ref[...], ds_ref[...] = grads(pl.multiple_of(c * KC, KC), KC, c)
                return carry

            p, ds = grads(plen, 2 * RB, last)
            p_ref[...], ds_ref[...] = grads(0, KC, 0)
            dcva[near, :] += jnp.dot(p, db, preferred_element_type=F32)
            dcka[near, :] += jnp.dot(ds, qb, preferred_element_type=F32)
            gq_ref[...] = lax.dot_general(ck[near, :], ds, TN, preferred_element_type=F32)
            lax.fori_loop(1, n_all, back, 0)
            products(n_all - 1)

            @pl.when(half)
            def _():
                at = pl.ds(tail, HC)
                p, ds = grads(tail, HC, n_all)
                dvt[at, :] += jnp.dot(p, db, preferred_element_type=F32)
                dkt[at, :] += jnp.dot(ds, qb, preferred_element_type=F32)
                gq_ref[...] += jnp.dot(kt_ref[:, at], ds, preferred_element_type=F32)

            gq = (gq_ref[...] * scale).T.astype(dq.dtype)
            for h in range(heads):
                dq[pl.ds(r0, RB), h * D:(h + 1) * D] = gq[h * RB:(h + 1) * RB, :]

        dq_copy(b).start()

    dck[...] = (dcka[...] * scale).astype(dck.dtype)
    dcv[...] = dcva[...].astype(dcv.dtype)
    stores = [pltpu.make_async_copy(dck, dck_out, out_sem.at[0]), pltpu.make_async_copy(dcv, dcv_out, out_sem.at[1])]
    for cp in stores:
        cp.start()
    for c in range(plen // KC):
        at = pl.ds(c * KC, KC)
        dk[at, :] = (dkt[at, :] * scale).astype(dk.dtype)
        dv[at, :] = dvt[at, :].astype(dv.dtype)
        for n, (src, dst) in enumerate(((dk, dk_out), (dv, dv_out))):
            cp = pltpu.make_async_copy(src.at[at, :], dst.at[at, :], out_sem.at[2 + 2 * c + n])
            cp.start()
            stores.append(cp)
    for b in range(rows // RB):
        dq_copy(b).wait()
    for cp in stores:
        cp.wait()


def attn_call(assign, lengths, offsets, q, do, ck, cv, kv):
    rows, width = q.shape
    plen = kv.shape[1]
    lanes = width // D * RB
    bf = jnp.bfloat16
    smem = pl.BlockSpec(memory_space=pltpu.SMEM)
    hbm = pl.BlockSpec(memory_space=pltpu.HBM)
    wide, thin, prompt = (rows, width), (rows, D), (plen, D)
    outs = (wide, thin, thin, prompt, prompt)
    return pl.pallas_call(
        attn_kernel,
        out_shape=tuple(jax.ShapeDtypeStruct(x, bf) for x in outs),
        in_specs=[smem] * 3 + [hbm] * 5,
        out_specs=[hbm] * 5,
        scratch_shapes=[pltpu.VMEM(x, bf) for x in (wide, wide, thin, thin, prompt, prompt) + outs] + [
            pltpu.SMEM((3, 8), jnp.int32),
            pltpu.VMEM((plen + 2 * RB, lanes), bf),
            pltpu.VMEM((plen + 2 * RB, lanes), F32),
            pltpu.VMEM((plen // KC + 1, 8, lanes), F32),
            pltpu.VMEM((plen, D), F32),
            pltpu.VMEM((plen, D), F32),
            pltpu.VMEM((rows, D), F32),
            pltpu.VMEM((rows, D), F32),
            pltpu.VMEM((KC, lanes), F32),
            pltpu.VMEM((KC, lanes), bf),
            pltpu.VMEM((KC, lanes), bf),
            pltpu.VMEM((D, lanes), F32),
            pltpu.VMEM((D, plen), bf),
            pltpu.SemaphoreType.DMA((6,)),
            pltpu.SemaphoreType.DMA((rows // RB,)),
            pltpu.SemaphoreType.DMA((2 + 2 * (plen // KC),)),
        ],
        compiler_params=pltpu.CompilerParams(vmem_limit_bytes=63 << 20),
    )(assign, lengths, offsets, q, do, ck, cv, kv)


def per_device(query, grad_out, continuation_key, continuation_value, prompt_key, shared_prompt_value, assign, lengths, offsets):
    prompt = gather(prompt_key, shared_prompt_value)
    query_grad, key_grad, value_grad, dk, dv = attn_call(
        assign, lengths, offsets, query, grad_out, continuation_key, continuation_value, prompt
    )
    prompt_key_grad, prompt_value_grad = reduce(dk, dv)
    return query_grad, key_grad, value_grad, prompt_key_grad, prompt_value_grad


def solution(mesh):
    rows = P("cand", "prefix")
    owned = P(("prefix", "cand"), None)
    return jax.shard_map(
        per_device,
        mesh=mesh,
        in_specs=(rows, rows, rows, rows, owned, owned, P(), P(), P()),
        out_specs=(rows, rows, rows, owned, owned),
        check_vma=False,
    )
```

```python
import functools
import math

import jax
import jax.numpy as jnp
from jax import lax
from jax.experimental import pallas as pl
from jax.experimental.pallas import tpu as pltpu
from jax.sharding import PartitionSpec as P

D = 128
MESH = pl.DeviceIdType.MESH
ALL = pl.ds(0, 8)
HEADS_FAR = [(2, 1), (2, 0), (1, 1), (3, 1), (1, 0), (3, 0), (0, 1), (0, 0)]
GROUPS = [
    [(2, dz, dy, dl) for dz in (1, 0) for dy, dl in HEADS_FAR],
    [(1, dz, dy, dl) for dz in (1, 0) for dy, dl in HEADS_FAR],
    [(3, dz, dy, dl) for dz in (1, 0) for dy, dl in HEADS_FAR],
    [(0, 1, dy, dl) for dy, dl in HEADS_FAR],
    [(0, 0, dy, dl) for dy, dl in HEADS_FAR[:-1]],
]


class Place:
    def __init__(self):
        self.p, self.c = lax.axis_index("prefix"), lax.axis_index("cand")
        self.x, self.zh, self.co = self.c // 4, (self.c // 2) % 2, self.c % 2
        self.zl, self.y = self.p // 4, self.p % 4
        self.partner = (self.p, self.c + 1 - 2 * self.co)

    def head(self, dy, dl):
        return ((self.zl + dl) % 2) * 4 + (self.y + dy) % 4

    def chip(self, dx, dz):
        return (self.x + dx) % 4, (self.zh + dz) % 2

    def peer(self, dx, dz, dy, dl):
        x, zh = self.chip(dx, dz)
        return (self.head(dy, dl), x * 4 + zh * 2 + self.co)


def greet(at):
    barrier = pltpu.get_barrier_semaphore()
    n = 1
    pl.semaphore_signal(barrier, inc=1, device_id=at.partner, device_id_type=MESH)
    for group in GROUPS:
        for offset in group:
            n += 1
            pl.semaphore_signal(barrier, inc=1, device_id=at.peer(*offset), device_id_type=MESH)
    pl.semaphore_wait(barrier, n)


def remote(src, dst, send, recv, peer):
    return pltpu.make_async_remote_copy(src_ref=src, dst_ref=dst, send_sem=send, recv_sem=recv, device_id=peer, device_id_type=MESH)


def columns(head):
    return pl.ds(pl.multiple_of(head * D, D), D)


def gather_kernel(pk, pv, full, stage, send, recv, send_near, recv_near, send_core, recv_core, own_sem):
    at = Place()
    staged = []
    for a, src in enumerate((pk, pv)):
        cp = pltpu.make_async_copy(src, stage.at[a], own_sem.at[a])
        cp.start()
        staged.append(cp)
    greet(at)
    for cp in staged:
        cp.wait()
    near = []
    for g, group in enumerate(GROUPS):
        for i, offset in enumerate(group):
            peer = at.peer(*offset)
            s, r = (send.at[g], recv.at[g]) if g < 4 else (send_near.at[i], recv_near.at[i])
            cp = remote(stage.at[:, :, columns(peer[0])], full.at[:, at.p, at.x, at.zh, at.co], s, r, peer)
            cp.start()
            if g == 4:
                near.append(cp)
    own = pltpu.make_async_copy(stage.at[:, :, columns(at.p)], full.at[:, at.p, at.x, at.zh, at.co], own_sem.at[2])
    own.start()
    regions = [(at.chip(2, 0)[0], pl.ds(0, 2)), (at.chip(3, 0)[0], pl.ds(0, 2)), (at.chip(1, 0)[0], pl.ds(0, 2)), (at.x, 1 - at.zh), (at.x, at.zh)]
    handed = []

    def hand(g):
        ref = full.at[:, ALL, regions[g][0], regions[g][1], at.co]
        cp = remote(ref, ref, send_core.at[g], recv_core.at[g], at.partner)
        cp.start()
        handed.append(cp)

    bulk = []
    for g in range(4):
        ref = full.at[:, ALL, regions[g][0], regions[g][1], at.co]
        cp = remote(ref, ref, send.at[g], recv.at[g], at.partner)
        cp.wait_recv()
        bulk.append(cp)
        hand(g)
    for cp in near:
        cp.wait_recv()
    own.wait()
    hand(4)
    for cp in handed:
        cp.wait_recv()
    for cp in bulk + near + handed:
        cp.wait_send()


def gather(pk, pv):
    rows = pk.shape[0]
    hbm = pl.BlockSpec(memory_space=pltpu.HBM)
    dma = lambda *s: pltpu.SemaphoreType.DMA(s)
    full = pl.pallas_call(
        gather_kernel,
        out_shape=jax.ShapeDtypeStruct((2, 8, 4, 2, 2, rows, D), pk.dtype),
        in_specs=[hbm] * 2,
        out_specs=hbm,
        scratch_shapes=[pltpu.VMEM((2, rows, 8 * D), pk.dtype), dma(4), dma(4), dma(7), dma(7), dma(5), dma(5), dma(3)],
        compiler_params=pltpu.CompilerParams(collective_id=0, has_side_effects=True),
    )(pk, pv)
    return full.reshape(2, -1, D)


def reduce_kernel(dk, dv, ok, ov, mine, other, part, came, send, recv, send_near, recv_near, send_core, recv_core, own_sem):
    at = Place()
    f32 = jnp.float32
    order = [at.chip(2, 0)[0], at.chip(1, 0)[0], at.chip(3, 0)[0], at.x]
    loads = []
    for i, x in enumerate(order):
        for a, src in enumerate((dk, dv)):
            cp = pltpu.make_async_copy(src.at[:, x, :, at.co], mine.at[a, i], own_sem.at[a, i])
            cp.start()
            loads.append(cp)
    greet(at)
    crossed = []
    for i, x in enumerate(order):
        for a, src in enumerate((dk, dv)):
            cp = remote(src.at[:, x, :, 1 - at.co], other.at[a, i], send_core.at[a, i], recv_core.at[a, i], at.partner)
            cp.start()
            crossed.append(cp)
    near = []
    slot = at.x * 2 + at.zh
    for i in range(4):
        for a in range(2):
            loads[2 * i + a].wait()
            crossed[2 * i + a].wait_recv()
            part[a, i] = (mine[a, i].astype(f32) + other[a, i].astype(f32)).astype(part.dtype)
            for g in ((i,) if i < 3 else (3, 4)):
                for j, offset in enumerate(GROUPS[g]):
                    peer = at.peer(*offset)
                    s, r = (send.at[a, g], recv.at[a, g]) if g < 4 else (send_near.at[a, j], recv_near.at[a, j])
                    zh = at.chip(0, offset[1])[1]
                    cp = remote(part.at[a, i, peer[0], zh], came.at[a, slot, :, columns(at.p)], s, r, peer)
                    cp.start()
                    if g == 4:
                        near.append(cp)
    own = []
    for a in range(2):
        cp = pltpu.make_async_copy(part.at[a, 3, at.p, at.zh], came.at[a, slot, :, columns(at.p)], own_sem.at[a, 4])
        cp.start()
        own.append(cp)
    bulk = []
    for g in range(4):
        for a in range(2):
            ref = mine.at[a, g] if g < 3 else mine.at[a, g, :, 0]
            cp = remote(ref, ref, send.at[a, g], recv.at[a, g], at.partner)
            cp.wait_recv()
            bulk.append(cp)
    for cp in near:
        cp.wait_recv()
    for cp in own:
        cp.wait()
    for a, out in enumerate((ok, ov)):
        total = came[a, 0].astype(f32)
        for s in range(1, 8):
            total += came[a, s].astype(f32)
        out[...] = total.astype(out.dtype)
    for cp in crossed + bulk + near:
        cp.wait_send()


def reduce(dk, dv):
    rows = dk.shape[0] // 128
    bf = dk.dtype
    shape = (8, 4, 2, 2, rows, D)
    out = jax.ShapeDtypeStruct((rows, 8 * D), bf)
    dma = lambda *s: pltpu.SemaphoreType.DMA(s)
    buf = pltpu.VMEM((2, 4, 8, 2, rows, D), bf)
    return pl.pallas_call(
        reduce_kernel,
        out_shape=(out, out),
        in_specs=[pl.BlockSpec(memory_space=pltpu.HBM)] * 2,
        out_specs=[pl.BlockSpec(memory_space=pltpu.VMEM)] * 2,
        scratch_shapes=[buf, buf, buf, pltpu.VMEM((2, 8, rows, 8 * D), bf),
                        dma(2, 4), dma(2, 4), dma(2, 7), dma(2, 7), dma(2, 4), dma(2, 4), dma(2, 5)],
        compiler_params=pltpu.CompilerParams(collective_id=1, has_side_effects=True, vmem_limit_bytes=56_000_000),
    )(dk.reshape(shape), dv.reshape(shape))


KC = 768
HC = 384
RB = 64
NEG = -1e30
NT = (((1,), (1,)), ((), ()))
TN = (((0,), (0,)), ((), ()))
F32 = jnp.float32


def groups(x):
    return x.reshape(x.shape[0] // 8, 8, x.shape[1])


def attn_kernel(assign, lengths, offsets, q_in, do_in, ck_in, cv_in, kv, dq_out, dck_out, dcv_out, dk_out, dv_out,
                q, do, ck, cv, k, v, dq, dck, dcv, dk, dv, slots, e_ref, dp_ref, mx_ref, dkt, dvt, dcka, dcva,
                t_ref, p_ref, ds_ref, gq_ref, kt_ref, in_sem, dq_sem, out_sem):
    rows, width = q.shape
    heads = width // D
    plen = k.shape[0]
    lanes = heads * RB
    scale = 1.0 / math.sqrt(D)
    cand = lax.axis_index("cand")

    loads = [
        pltpu.make_async_copy(src, dst, in_sem.at[n])
        for n, (src, dst) in enumerate(((kv.at[0], k), (kv.at[1], v), (q_in, q), (do_in, do), (ck_in, ck), (cv_in, cv)))
    ]
    for cp in loads:
        cp.start()

    def place_rows(i, carry):
        slot, start = carry
        slots[0, slot] = start
        slots[1, slot] = start + lengths[i]
        slots[2, slot] = offsets[i]
        hit = assign[i] == cand
        return (jnp.where(hit, slot + 1, slot), jnp.where(hit, start + lengths[i], start))

    lax.fori_loop(0, assign.shape[0], place_rows, (jnp.int32(0), jnp.int32(0)), unroll=8)
    dkt[...] = jnp.zeros_like(dkt)
    dvt[...] = jnp.zeros_like(dvt)
    dcka[...] = jnp.zeros_like(dcka)
    dcva[...] = jnp.zeros_like(dcva)
    loads[0].wait()

    @pl.loop(0, plen // KC)
    def _(c):
        at = pl.multiple_of(c * KC, KC)
        kt_ref[:, pl.ds(at, KC)] = k[pl.ds(at, KC), :].T

    for cp in loads[1:]:
        cp.wait()

    def dq_copy(b):
        band = pl.ds(pl.multiple_of(b * RB, RB), RB)
        return pltpu.make_async_copy(dq.at[band, :], dq_out.at[band, :], dq_sem.at[b])

    @pl.loop(0, rows // RB)
    def _(b):
        r0 = pl.multiple_of(b * RB, RB)
        row = r0 + (lax.broadcasted_iota(jnp.int32, (1, lanes), 1) & (RB - 1))
        off = jnp.zeros((1, lanes), jnp.int32)
        first = jnp.zeros((1, lanes), jnp.int32) + rows
        max_off = jnp.int32(0)
        min_off = jnp.int32(plen)
        for i in range(4):
            lo, hi, n = slots[0, i], slots[1, i], slots[2, i]
            inside = (row >= lo) & (row < hi)
            off = jnp.where(inside, n, off)
            first = jnp.where(inside, lo, first)
            meets = (lo < r0 + RB) & (hi > r0)
            max_off = jnp.maximum(max_off, jnp.where(meets, n, 0))
            min_off = jnp.minimum(min_off, jnp.where(meets, n, plen))
        valid = off > 0
        n_all = (max_off + KC - HC - 1) // KC
        half = max_off > n_all * KC
        n_free = jnp.minimum(min_off // KC, n_all)
        off = jnp.where(valid, off, plen)

        @pl.when(max_off == 0)
        def _():
            dq[pl.ds(r0, RB), :] = jnp.zeros((RB, width), dq.dtype)

        @pl.when(max_off > 0)
        def _():
            qb = jnp.concatenate([q[pl.ds(r0, RB), h * D:(h + 1) * D] for h in range(heads)], axis=0)
            db = jnp.concatenate([do[pl.ds(r0, RB), h * D:(h + 1) * D] for h in range(heads)], axis=0)
            w0 = pl.multiple_of(jnp.maximum(r0 - RB, 0), RB)

            def raw(kk, mask):
                t = lax.dot_general(kk, qb, NT, preferred_element_type=F32) * scale
                return t if mask is None else jnp.where(mask, t, NEG)

            def weigh(vv, at, slot, n, old, m, l, d):
                e = jnp.exp(groups(t_ref[pl.ds(0, n), :]) - m[None])
                mx_ref[slot] = m
                e_ref[pl.ds(at, n), :] = e.reshape(n, lanes).astype(jnp.bfloat16)
                dp = lax.dot_general(vv, db, NT, preferred_element_type=F32)
                dp_ref[pl.ds(at, n), :] = dp
                fade = jnp.exp(old - m)
                return l * fade + jnp.sum(e, axis=0), d * fade + jnp.sum(e * groups(dp), axis=0)

            def mask_at(at):
                return at + lax.broadcasted_iota(jnp.int32, (KC, lanes), 0) < off

            def piece(ref, c):
                return ref[pl.ds(pl.multiple_of(c * KC, KC), KC), :]

            def step_to(c, mask, carry):
                old, m, l, d = carry
                t = raw(piece(k, c), mask)
                l, d = weigh(piece(v, c - 1), pl.multiple_of((c - 1) * KC, KC), c - 1, KC, old, m, l, d)
                t_ref[...] = t
                return m, jnp.maximum(m, jnp.max(groups(t), axis=0)), l, d

            zero = jnp.zeros((8, lanes), F32)
            low = jnp.full((8, lanes), NEG, F32)
            near = pl.ds(w0, 2 * RB)
            last = plen // KC
            key = w0 + lax.broadcasted_iota(jnp.int32, (2 * RB, lanes), 0)
            first_t = raw(ck[near, :], (key >= first) & (key <= row))
            m = jnp.max(groups(first_t), axis=0)
            t_ref[pl.ds(0, 2 * RB), :] = first_t
            t = raw(piece(k, 0), None)
            l, d = weigh(cv[near, :], plen, last, 2 * RB, low, m, zero, zero)
            t_ref[...] = t
            carry = (m, jnp.maximum(m, jnp.max(groups(t), axis=0)), l, d)
            turn = jnp.maximum(n_free, 1)
            carry = lax.fori_loop(1, turn, lambda c, x: step_to(c, None, x), carry)
            carry = lax.fori_loop(turn, n_all, lambda c, x: step_to(c, mask_at(c * KC), x), carry)
            old, m, l, d = carry
            tail = pl.multiple_of(n_all * KC, KC)

            def end_half(_):
                t = raw(k[pl.ds(tail, HC), :], tail + lax.broadcasted_iota(jnp.int32, (HC, lanes), 0) < off)
                l1, d1 = weigh(piece(v, n_all - 1), pl.multiple_of((n_all - 1) * KC, KC), n_all - 1, KC, old, m, l, d)
                t_ref[pl.ds(0, HC), :] = t
                m1 = jnp.maximum(m, jnp.max(groups(t), axis=0))
                l1, d1 = weigh(v[pl.ds(tail, HC), :], tail, n_all, HC, m, m1, l1, d1)
                return m1, l1, d1

            def end_whole(_):
                l1, d1 = weigh(piece(v, n_all - 1), pl.multiple_of((n_all - 1) * KC, KC), n_all - 1, KC, old, m, l, d)
                return m, l1, d1

            m, l, d = lax.cond(half, end_half, end_whole, 0)

            top = jnp.max(m, axis=0, keepdims=True)
            fade = jnp.exp(m - top)
            inv = jnp.where(valid, 1.0 / jnp.sum(l * fade, axis=0, keepdims=True), 0.0)
            delta = jnp.sum(d * fade, axis=0, keepdims=True) * inv
            delta = jnp.broadcast_to(delta, (8, lanes))

            def grads(at, n, slot):
                g = (jnp.exp(mx_ref[slot] - top) * inv).astype(jnp.bfloat16)
                g = jnp.concatenate([g, g], axis=0)
                p = (e_ref[pl.ds(at, n), :].reshape(n // 16, 16, lanes) * g[None]).reshape(n, lanes)
                u = groups(dp_ref[pl.ds(at, n), :]) - delta[None]
                return p, p * u.reshape(n, lanes).astype(jnp.bfloat16)

            def products(c):
                at = pl.multiple_of(c * KC, KC)
                p, ds = p_ref[...], ds_ref[...]
                dvt[pl.ds(at, KC), :] += jnp.dot(p, db, preferred_element_type=F32)
                dkt[pl.ds(at, KC), :] += jnp.dot(ds, qb, preferred_element_type=F32)
                gq_ref[...] += jnp.dot(kt_ref[:, pl.ds(at, KC)], ds, preferred_element_type=F32)

            def back(c, carry):
                products(c - 1)
                p_ref[...], ds_ref[...] = grads(pl.multiple_of(c * KC, KC), KC, c)
                return carry

            p, ds = grads(plen, 2 * RB, last)
            p_ref[...], ds_ref[...] = grads(0, KC, 0)
            dcva[near, :] += jnp.dot(p, db, preferred_element_type=F32)
            dcka[near, :] += jnp.dot(ds, qb, preferred_element_type=F32)
            gq_ref[...] = lax.dot_general(ck[near, :], ds, TN, preferred_element_type=F32)
            lax.fori_loop(1, n_all, back, 0)
            products(n_all - 1)

            @pl.when(half)
            def _():
                at = pl.ds(tail, HC)
                p, ds = grads(tail, HC, n_all)
                dvt[at, :] += jnp.dot(p, db, preferred_element_type=F32)
                dkt[at, :] += jnp.dot(ds, qb, preferred_element_type=F32)
                gq_ref[...] += jnp.dot(kt_ref[:, at], ds, preferred_element_type=F32)

            gq = (gq_ref[...] * scale).T.astype(dq.dtype)
            for h in range(heads):
                dq[pl.ds(r0, RB), h * D:(h + 1) * D] = gq[h * RB:(h + 1) * RB, :]

        dq_copy(b).start()

    dck[...] = (dcka[...] * scale).astype(dck.dtype)
    dcv[...] = dcva[...].astype(dcv.dtype)
    stores = [pltpu.make_async_copy(dck, dck_out, out_sem.at[0]), pltpu.make_async_copy(dcv, dcv_out, out_sem.at[1])]
    for cp in stores:
        cp.start()
    for c in range(plen // KC):
        at = pl.ds(c * KC, KC)
        dk[at, :] = (dkt[at, :] * scale).astype(dk.dtype)
        dv[at, :] = dvt[at, :].astype(dv.dtype)
        for n, (src, dst) in enumerate(((dk, dk_out), (dv, dv_out))):
            cp = pltpu.make_async_copy(src.at[at, :], dst.at[at, :], out_sem.at[2 + 2 * c + n])
            cp.start()
            stores.append(cp)
    for b in range(rows // RB):
        dq_copy(b).wait()
    for cp in stores:
        cp.wait()


def attn_call(assign, lengths, offsets, q, do, ck, cv, kv):
    rows, width = q.shape
    plen = kv.shape[1]
    lanes = width // D * RB
    bf = jnp.bfloat16
    smem = pl.BlockSpec(memory_space=pltpu.SMEM)
    hbm = pl.BlockSpec(memory_space=pltpu.HBM)
    wide, thin, prompt = (rows, width), (rows, D), (plen, D)
    outs = (wide, thin, thin, prompt, prompt)
    return pl.pallas_call(
        attn_kernel,
        out_shape=tuple(jax.ShapeDtypeStruct(x, bf) for x in outs),
        in_specs=[smem] * 3 + [hbm] * 5,
        out_specs=[hbm] * 5,
        scratch_shapes=[pltpu.VMEM(x, bf) for x in (wide, wide, thin, thin, prompt, prompt) + outs] + [
            pltpu.SMEM((3, 8), jnp.int32),
            pltpu.VMEM((plen + 2 * RB, lanes), bf),
            pltpu.VMEM((plen + 2 * RB, lanes), F32),
            pltpu.VMEM((plen // KC + 1, 8, lanes), F32),
            pltpu.VMEM((plen, D), F32),
            pltpu.VMEM((plen, D), F32),
            pltpu.VMEM((rows, D), F32),
            pltpu.VMEM((rows, D), F32),
            pltpu.VMEM((KC, lanes), F32),
            pltpu.VMEM((KC, lanes), bf),
            pltpu.VMEM((KC, lanes), bf),
            pltpu.VMEM((D, lanes), F32),
            pltpu.VMEM((D, plen), bf),
            pltpu.SemaphoreType.DMA((6,)),
            pltpu.SemaphoreType.DMA((rows // RB,)),
            pltpu.SemaphoreType.DMA((2 + 2 * (plen // KC),)),
        ],
        compiler_params=pltpu.CompilerParams(vmem_limit_bytes=63 << 20),
    )(assign, lengths, offsets, q, do, ck, cv, kv)


def per_device(query, grad_out, continuation_key, continuation_value, prompt_key, shared_prompt_value, assign, lengths, offsets):
    prompt = gather(prompt_key, shared_prompt_value)
    query_grad, key_grad, value_grad, dk, dv = attn_call(
        assign, lengths, offsets, query, grad_out, continuation_key, continuation_value, prompt
    )
    prompt_key_grad, prompt_value_grad = reduce(dk, dv)
    return query_grad, key_grad, value_grad, prompt_key_grad, prompt_value_grad


def solution(mesh):
    rows = P("cand", "prefix")
    owned = P(("prefix", "cand"), None)
    return jax.shard_map(
        per_device,
        mesh=mesh,
        in_specs=(rows, rows, rows, rows, owned, owned, P(), P(), P()),
        out_specs=(rows, rows, rows, owned, owned),
        check_vma=False,
    )
```
